32 devices in a mesh: groups: 2 (over x), seq: 16 (over z, y, core).
Axes of the slice: x: 2, y: 2, z: 4, core: 2. Of those that a mesh axis runs over, the one named last changes fastest.
Arguments:
- grad_out: bfloat16 [4096, 4096], P(None, ('groups', 'seq')), parts along dimension 1, may hold values from -6 to 6
- query: bfloat16 [4096, 4096], P(None, ('groups', 'seq')), parts along dimension 1, may hold values from -6 to 6
- key: bfloat16 [4096, 4096], P(None, ('groups', 'seq')), parts along dimension 1, may hold values from -6 to 6
- value: bfloat16 [4096, 4096], P(None, ('groups', 'seq')), parts along dimension 1, may hold values from -6 to 6
- conv_out: bfloat16 [4096, 4096], P(None, ('groups', 'seq')), parts along dimension 1, may hold values from -6 to 6
- channel_filter: int32 [4096], replicated, may hold values from 0 to 127, as said below
- decay_rate: float32 [128, 16], replicated, may hold values from 0.01 to 68
- twist: float32 [128, 16], replicated, may hold values from -3 to 3
- residues: float32 [2, 128, 16], replicated, may hold values from -1.5 to 1.5
Outputs:
- grad_query: bfloat16 [4096, 4096], P(None, ('groups', 'seq')), parts along dimension 1
- grad_key: bfloat16 [4096, 4096], P(None, ('groups', 'seq')), parts along dimension 1
- grad_value: bfloat16 [4096, 4096], P(None, ('groups', 'seq')), parts along dimension 1
- grad_log_rate: float32 [256, 16], P('groups'), parts along dimension 0
- grad_twist: float32 [256, 16], P('groups'), parts along dimension 0
- grad_residues: float32 [4, 128, 16], P('groups'), parts along dimension 0
The draws below stay inside these ranges and needn't reach their ends.
There are 2 independent parts, one for each index of `groups`. The reference program is written for one: setup_inputs(seed, part) draws one part's arguments, and reference() takes and returns one part's arrays. A program takes and returns all parts, laid end to end along the dimension named above; an argument that names none is the same for every part. Nothing has to cross between parts.
Inputs may be any that keep to these rules, and one draw needn't show every extreme that they name: `channel_filter`: each of the 128 filters is used by exactly 32 channels.
All inputs are finite; a program needn't handle non-finite values.
Results may differ from the reference program's by a relative error of at most 0.0051.
Values sent between devices are 32-bit elements; how exact they have to be, the bound alone decides.
No kernel may reach another device: no remote copies, remote signals or barrier semaphores. Data moves between devices by JAX's collectives and lax.ppermute only.
A program may use at most 384 MiB of HBM per device.

```python
import math
import jax
import jax.numpy as jnp
from jax import lax

D = 4096
FILTERS = 128
MODES = 16
LENGTH = 2048


def draw_channel_filter(key, part):
    shuffled = jax.random.permutation(jax.random.fold_in(key, 11), D)
    return (shuffled % FILTERS).astype(jnp.int32)


def block_levels(own_key, extent, split, low, top_value):
    def one(dim, shards_of):
        heights = jax.random.uniform(jax.random.fold_in(jax.random.fold_in(own_key, 6), dim), (shards_of,), jnp.float32, low / len(split), top_value / len(split))
        return jnp.repeat(jnp.exp(heights), extent[dim] // shards_of).reshape((-1,) + (1,) * (len(extent) - dim - 1))

    gain = one(*split[0])
    for cut in split[1:]:
        gain = gain * one(*cut)
    return gain


def gaussian(own_key, extent, width, bound, split=(), kind=jnp.bfloat16):
    drawn = width * jax.random.normal(own_key, extent, jnp.float32)
    if split:
        drawn = drawn * block_levels(own_key, extent, split, -0.22, 0.18)
    return jnp.clip(drawn, -bound, bound).astype(kind)


def setup_inputs(seed: int = 0, part: int = 0) -> dict:
    seeds = jax.random.split(jax.random.key(seed), 10)
    part_splits = jax.random.split(jax.random.fold_in(seeds[9], part), 10)
    grad_out = gaussian(part_splits[0], (D, LENGTH), 1.0, 6.0, ((1, 16),))
    query = gaussian(part_splits[1], (D, LENGTH), 1.0, 6.0, ((1, 16),))
    key = gaussian(part_splits[2], (D, LENGTH), 1.0, 6.0, ((1, 16),))
    value = gaussian(part_splits[3], (D, LENGTH), 1.0, 6.0, ((1, 16),))
    conv_out = gaussian(part_splits[4], (D, LENGTH), 1.0, 6.0, ((1, 16),))
    channel_filter = draw_channel_filter(jax.random.fold_in(seeds[9], 71), part)
    decay_rate = jnp.clip(jnp.exp(jax.random.uniform(seeds[6], (FILTERS, MODES), jnp.float32, math.log(0.01), math.log(68.0))), 0.01, 68.0)
    twist = jnp.clip(jax.random.uniform(seeds[7], (FILTERS, MODES), jnp.float32, -3.0, 3.0), -3.0, 3.0)
    residues = gaussian(seeds[8], (2, FILTERS, MODES), 0.25, 1.5, (), jnp.float32)
    return dict(grad_out=grad_out, query=query, key=key, value=value, conv_out=conv_out, channel_filter=channel_filter, decay_rate=decay_rate, twist=twist, residues=residues)


def complex_product(a_real, a_imag, b_real, b_imag):
    return (a_real * b_real - a_imag * b_imag, a_real * b_imag + a_imag * b_real)

def mode_tables(decay_rate, twist, residues, length):
    rho = decay_rate / length
    angle = twist * rho
    scale = jnp.sqrt(1.0 - jnp.exp(-2.0 * rho))
    return (rho, angle, residues[0] * scale, residues[1] * scale)

def param_grads(decay_rate, twist, residues, length, a_real, a_imag, w_real, w_imag):
    rho_fixed, angle_fixed, res_real, res_imag = mode_tables(decay_rate, twist, residues, length)
    rw_real, rw_imag = complex_product(res_real, res_imag, w_real, w_imag)

    def objective(log_rate, twist_val, residue_val):
        rho, angle, rr_val, ri_val = mode_tables(jnp.exp(log_rate), twist_val, residue_val, length)
        magnitude = jnp.exp(-rho)
        first = jnp.sum(rr_val * a_real - ri_val * a_imag)
        second = jnp.sum(rw_real * magnitude * jnp.cos(angle) - rw_imag * magnitude * jnp.sin(angle))
        return first + second
    return jax.grad(objective, argnums=(0, 1, 2))(jnp.log(decay_rate), twist, residues)

def reference(grad_out, query, key, value, conv_out, channel_filter, decay_rate, twist, residues):
    highest = lax.Precision.HIGHEST
    grad_query = (grad_out.astype(jnp.float32) * conv_out.astype(jnp.float32)).astype(jnp.bfloat16)
    mixed = lax.optimization_barrier((key.astype(jnp.float32) * value.astype(jnp.float32)).astype(jnp.bfloat16))
    gate_grad = lax.optimization_barrier((grad_out.astype(jnp.float32) * query.astype(jnp.float32)).astype(jnp.bfloat16))
    members = D // FILTERS
    order = jnp.argsort(channel_filter, stable=True).astype(jnp.int32)
    mixed_grouped = mixed.astype(jnp.float32)[order].reshape(FILTERS, members, LENGTH)
    gate_grouped = gate_grad.astype(jnp.float32)[order].reshape(FILTERS, members, LENGTH)
    rho, angle, res_real, res_imag = mode_tables(decay_rate, twist, residues, LENGTH)
    steps = jnp.arange(LENGTH, dtype=jnp.float32)
    padded = 2 * LENGTH

    def per_filter(inputs):
        mixed_f, gate_f, rho_f, angle_f, rr_f, ri_f = inputs
        magnitude = jnp.exp(-rho_f[:, None] * steps[None, :])
        pow_real = magnitude * jnp.cos(angle_f[:, None] * steps[None, :])
        pow_imag = magnitude * jnp.sin(angle_f[:, None] * steps[None, :])
        filt = lax.optimization_barrier(jnp.sum(rr_f[:, None] * pow_real - ri_f[:, None] * pow_imag, axis=0))
        gate_spec = jnp.fft.rfft(gate_f, n=padded, axis=-1)
        mixed_spec = jnp.fft.rfft(mixed_f, n=padded, axis=-1)
        filt_spec = jnp.fft.rfft(filt, n=padded)
        conv_grad = jnp.fft.irfft(gate_spec * jnp.conj(filt_spec)[None, :], n=padded, axis=-1)[:, :LENGTH]
        lagged = jnp.fft.irfft(lax.optimization_barrier(jnp.sum(gate_spec * jnp.conj(mixed_spec), axis=0)), n=padded)[:LENGTH]
        conv_grad = conv_grad.astype(jnp.float32)
        lagged = lagged.astype(jnp.float32)
        shifted = steps - 1.0
        magnitude_d = steps[None, :] * jnp.exp(-rho_f[:, None] * shifted[None, :])
        der_real = magnitude_d * jnp.cos(angle_f[:, None] * shifted[None, :])
        der_imag = magnitude_d * jnp.sin(angle_f[:, None] * shifted[None, :])
        a_real = jnp.dot(pow_real, lagged, precision=highest)
        a_imag = jnp.dot(pow_imag, lagged, precision=highest)
        w_real = jnp.dot(der_real, lagged, precision=highest)
        w_imag = jnp.dot(der_imag, lagged, precision=highest)
        return (conv_grad, a_real, a_imag, w_real, w_imag)
    conv_grouped, a_real, a_imag, w_real, w_imag = lax.map(per_filter, (mixed_grouped, gate_grouped, rho, angle, res_real, res_imag))
    conv_grad = jnp.zeros((D, LENGTH), jnp.float32).at[order].set(conv_grouped.reshape(D, LENGTH))
    grad_key = (conv_grad * value.astype(jnp.float32)).astype(jnp.bfloat16)
    grad_value = (conv_grad * key.astype(jnp.float32)).astype(jnp.bfloat16)
    grad_log_rate, grad_twist, grad_residues = param_grads(decay_rate, twist, residues, LENGTH, a_real, a_imag, w_real, w_imag)
    return (grad_query, grad_key, grad_value, grad_log_rate, grad_twist, grad_residues)
```

```python
import functools

import jax
import jax.numpy as jnp
from jax import lax
from jax.experimental import pallas as pl
from jax.experimental.pallas import tpu as pltpu
from jax.sharding import PartitionSpec as P

F32 = jnp.float32
BF16 = jnp.bfloat16
LANES = 128


def complex_product(a_real, a_imag, b_real, b_imag):
    return (a_real * b_real - a_imag * b_imag, a_real * b_imag + a_imag * b_real)


def split(x):
    hi = x.astype(BF16)
    return hi, (x - hi.astype(F32)).astype(BF16)


def dot(lhs, rhs, contract):
    return lax.dot_general(lhs, rhs, (contract, ((), ())), preferred_element_type=F32)


NN = ((1,), (0,))
NT = ((1,), (1,))
TN = ((0,), (0,))


def place_kernel(per_filter, filter_ref, pos_ref):
    rows = lax.broadcasted_iota(jnp.int32, (LANES, LANES), 0)
    cols = lax.broadcasted_iota(jnp.int32, (LANES, LANES), 1)
    before = (rows < cols).astype(F32).astype(BF16)
    ones = jnp.ones((LANES, LANES), BF16)
    pair = jnp.concatenate([before, ones], axis=1)
    seen = (rows * per_filter).astype(F32)
    for block in range(filter_ref.shape[0]):
        hot = rows == filter_ref[block : block + 1, :]
        counts = dot(hot.astype(F32).astype(BF16), pair, NN)
        place = jnp.where(hot, counts[:, :LANES] + seen, 0.0)
        pos_ref[block : block + 1, :] = jnp.sum(place, axis=0, keepdims=True).astype(jnp.int32)
        seen = seen + counts[:, LANES:]


def powers(re_ref, im_ref, group, backward):
    low = slice(8, 16) if backward else slice(0, 8)
    low_re, low_im = re_ref[group, low, :], im_ref[group, low, :]
    real, imag = [], []
    for a in range(16):
        row = 16 + (15 - a if backward else a)
        high_re, high_im = re_ref[group, row : row + 1, :], im_ref[group, row : row + 1, :]
        r, i = complex_product(high_re, high_im, low_re, low_im)
        real.append(r)
        imag.append(i)
    return jnp.concatenate(real, axis=0), jnp.concatenate(imag, axis=0)


def stacked(real, imag):
    hi, lo = split(jnp.concatenate([real, imag], axis=1))
    return jnp.concatenate([hi, lo], axis=0)


def own_filter(rows, lanes, members, modes):
    row = lax.broadcasted_iota(jnp.int32, (rows, lanes), 0) // members
    lane = (lax.broadcasted_iota(jnp.int32, (rows, lanes), 1) % LANES) // modes
    return row == lane


def mode_sum(data, table, members, modes):
    out = dot(jnp.concatenate([data, data], axis=1), table, NN)
    lane = (lax.broadcasted_iota(jnp.int32, (members, 2 * LANES), 1) % LANES) // modes
    total = jnp.zeros((members, 2 * LANES), F32)
    for f in range(data.shape[0] // members):
        total = jnp.where(lane == f, out[f * members : (f + 1) * members], total)
    return total


def states_kernel(
    members, modes, pos_ref, go_ref, q_ref, k_ref, v_ref, re_ref, im_ref,
    gate_ref, mixed_ref, y_ref, x_ref, natural_g, natural_m, grouped_g, grouped_m,
):
    channels = go_ref.shape[0]
    tile = 256

    @pl.loop(0, channels // tile)
    def _(i):
        at = pl.ds(pl.multiple_of(i * tile, tile), tile)
        gate = (go_ref[at, :].astype(F32) * q_ref[at, :].astype(F32)).astype(BF16)
        mixed = (k_ref[at, :].astype(F32) * v_ref[at, :].astype(F32)).astype(BF16)
        natural_g[at, :] = gate.astype(F32)
        natural_m[at, :] = mixed.astype(F32)

    @pl.loop(0, channels // 16)
    def _(i):
        base = pl.multiple_of(i * 16, 16)
        for u in range(16):
            to = pos_ref[base + u]
            grouped_g[pl.ds(to, 1), :] = natural_g[pl.ds(base + u, 1), :]
            grouped_m[pl.ds(to, 1), :] = natural_m[pl.ds(base + u, 1), :]

    size = (LANES // modes) * members

    @pl.loop(0, channels // size)
    def _(g):
        at = pl.ds(pl.multiple_of(g * size, size), size)
        gate = grouped_g[at, :].astype(BF16)
        mixed = grouped_m[at, :].astype(BF16)
        gate_ref[at, :] = gate
        mixed_ref[at, :] = mixed
        y = mode_sum(gate, stacked(*powers(re_ref, im_ref, g, False)), members, modes)
        x = mode_sum(mixed, stacked(*powers(re_ref, im_ref, g, True)), members, modes)
        y_ref[g, 0], y_ref[g, 1] = y[:, :LANES], y[:, LANES:]
        x_ref[g, 0], x_ref[g, 1] = x[:, :LANES], x[:, LANES:]


def local_kernel(
    members, modes, gate_ref, mixed_ref, re_ref, im_ref, rr_ref, ri_ref,
    conv_ref, v_ref, w_ref, sums_ref, toe, lag,
):
    per = LANES // modes
    head_re, head_im = powers(re_ref, im_ref, 0, False)
    back_re, back_im = powers(re_ref, im_ref, 0, True)
    step = lax.broadcasted_iota(jnp.int32, (LANES, LANES), 0).astype(F32)
    gate, mixed = gate_ref[...], mixed_ref[...]
    der = stacked(step * head_re, step * head_im)
    v = mode_sum(gate, der, members, modes)
    span = float(LANES)
    w = mode_sum(
        mixed, stacked((span - step) * back_re, (span - step) * back_im), members, modes
    )
    v_ref[0, 0], v_ref[0, 1] = v[:, :LANES], v[:, LANES:]
    w_ref[0, 0], w_ref[0, 1] = w[:, :LANES], w[:, LANES:]
    head = stacked(head_re, head_im)
    head_hi, head_lo = head[:LANES], head[LANES:]
    own8 = own_filter(per, 2 * LANES, 1, modes)
    res = jnp.concatenate([rr_ref[0], -ri_ref[0]], axis=1)
    res_hi, res_lo = split(jnp.where(own8, res, 0.0))
    filt = dot(res_hi, head_hi, NT) + dot(res_lo, head_hi, NT) + dot(res_hi, head_lo, NT)
    row = lax.broadcasted_iota(jnp.int32, (LANES, LANES), 0)
    col = lax.broadcasted_iota(jnp.int32, (LANES, LANES), 1)
    causal = col >= row
    mirror = (row + col == LANES - 1).astype(F32).astype(BF16)
    mirrored = dot(mixed, mirror, NN).astype(BF16)
    for f in range(per):
        at = slice(f * members, (f + 1) * members)
        wide = jnp.broadcast_to(filt[f : f + 1, :], (LANES, LANES))
        shifted = pltpu.roll(wide, 0, 1, stride=1, stride_axis=0)
        hi, lo = split(jnp.where(causal, shifted, 0.0))
        gate_f = gate[at]
        conv_ref[at, :] = dot(gate_f, hi, NT) + dot(gate_f, lo, NT)
        corr = jnp.where(row + col >= LANES - 1, dot(mirrored[at], gate_f, TN), 0.0)
        aligned = pltpu.roll(corr, 1, 1, stride=1, stride_axis=0)
        lag[f : f + 1, :] = jnp.sum(aligned, axis=0, keepdims=True)
    lag_hi, lag_lo = split(lag[...])
    for which, table in enumerate((head, der)):
        hi, lo = table[:LANES], table[LANES:]
        out = dot(lag_hi, hi, NN) + dot(lag_lo, hi, NN) + dot(lag_hi, lo, NN)
        out = jnp.sum(jnp.where(own8, out, 0.0), axis=0, keepdims=True)
        sums_ref[0, 2 * which : 2 * which + 1, :] = out[:, :LANES]
        sums_ref[0, 2 * which + 1 : 2 * which + 2, :] = out[:, LANES:]


def sums_kernel(
    x_ref, w_ref, v_ref, yin_ref, xin_ref, pr_ref, pi_ref, local_ref, out_ref
):
    def member_sum(pair):
        return [jnp.sum(part, axis=0, keepdims=True) for part in pair]

    for g in range(x_ref.shape[0]):
        yin = (yin_ref[g, 0], yin_ref[g, 1])
        xin = (xin_ref[g, 0], xin_ref[g, 1])
        a = member_sum(complex_product(x_ref[g, 0], x_ref[g, 1], *yin))
        c1 = member_sum(complex_product(w_ref[g, 0], w_ref[g, 1], *yin))
        c2 = member_sum(complex_product(v_ref[g, 0], v_ref[g, 1], *xin))
        c3 = member_sum(complex_product(*xin, *yin))
        c3 = complex_product(pr_ref[g : g + 1, :], pi_ref[g : g + 1, :], *c3)
        out_ref[0, g : g + 1, :] = local_ref[g, 0:1, :] + a[0]
        out_ref[1, g : g + 1, :] = local_ref[g, 1:2, :] + a[1]
        span = float(LANES)
        out_ref[2, g : g + 1, :] = local_ref[g, 2:3, :] + c1[0] + c2[0] + span * c3[0]
        out_ref[3, g : g + 1, :] = local_ref[g, 3:4, :] + c1[1] + c2[1] + span * c3[1]


def finish_kernel(
    members, modes, pos_ref, conv_ref, yin_ref, re_ref, im_ref, rr_ref, ri_ref, k_ref, v_ref,
    gk_ref, gv_ref, grouped, natural,
):
    channels = conv_ref.shape[0]
    per = LANES // modes
    size = per * members

    @pl.loop(0, channels // size)
    def _(g):
        at = pl.ds(pl.multiple_of(g * size, size), size)
        back_re, back_im = powers(re_ref, im_ref, g, True)
        rr, ri = rr_ref[g], ri_ref[g]
        coef_re, coef_im = complex_product(rr, ri, back_re, back_im)
        coef_hi, coef_lo = split(jnp.concatenate([coef_re, -coef_im], axis=1))
        yin = jnp.concatenate([yin_ref[g, 0], yin_ref[g, 1]], axis=1)
        lane = (lax.broadcasted_iota(jnp.int32, (members, 2 * LANES), 1) % LANES) // modes
        wide = jnp.concatenate([jnp.where(lane == f, yin, 0.0) for f in range(per)], axis=0)
        hi, lo = split(wide)
        cross = dot(hi, coef_hi, NT) + dot(lo, coef_hi, NT) + dot(hi, coef_lo, NT)
        grouped[at, :] = conv_ref[at, :] + cross

    @pl.loop(0, channels // 16)
    def _(i):
        base = pl.multiple_of(i * 16, 16)
        for u in range(16):
            natural[pl.ds(base + u, 1), :] = grouped[pl.ds(pos_ref[base + u], 1), :]

    tile = 256

    @pl.loop(0, channels // tile)
    def _(i):
        at = pl.ds(pl.multiple_of(i * tile, tile), tile)
        conv = natural[at, :]
        gk_ref[at, :] = (conv * v_ref[at, :].astype(F32)).astype(BF16)
        gv_ref[at, :] = (conv * k_ref[at, :].astype(F32)).astype(BF16)


def vmem(n):
    return [pl.BlockSpec(memory_space=pltpu.VMEM)] * n


SMEM = pl.BlockSpec(memory_space=pltpu.SMEM)
PARAMS = pltpu.CompilerParams(vmem_limit_bytes=48 << 20)


def swap(value, bit):
    count = lax.axis_size("seq")
    return lax.ppermute(value, "seq", [(i, i ^ bit) for i in range(count)])


def body(grad_out, query, key, value, conv_out, channel_filter, decay_rate, twist, residues):
    channels, positions = grad_out.shape
    filters, modes = decay_rate.shape
    members = channels // filters
    per = LANES // modes
    groups = filters // per
    count = lax.axis_size("seq")
    me = lax.axis_index("seq")
    length = positions * count
    shape = jax.ShapeDtypeStruct

    pos = pl.pallas_call(
        functools.partial(place_kernel, members),
        out_shape=shape((channels // LANES, LANES), jnp.int32),
        in_specs=vmem(1),
        out_specs=vmem(1)[0],
    )(channel_filter.reshape(channels // LANES, LANES)).reshape(channels)

    small = jnp.stack([decay_rate, twist, residues[0], residues[1]]).reshape(4, groups, LANES)
    rho = small[0] / length
    angle = small[1] * rho
    scale = jnp.sqrt(1.0 - jnp.exp(-2.0 * rho))
    rr, ri = small[2] * scale, small[3] * scale

    def power(steps):
        mag = jnp.exp(-rho[:, None, :] * steps[None, :, None])
        phase = angle[:, None, :] * steps[None, :, None]
        return mag * jnp.cos(phase), mag * jnp.sin(phase)

    low = jnp.arange(8, dtype=F32)
    steps = jnp.concatenate([low, 8.0 - low, 8.0 * jnp.arange(16, dtype=F32)])
    tab_re, tab_im = power(steps)

    state = shape((groups, 2, members, LANES), F32)
    gate, mixed, y, x = pl.pallas_call(
        functools.partial(states_kernel, members, modes),
        out_shape=(
            shape((channels, positions), BF16), shape((channels, positions), BF16), state, state,
        ),
        in_specs=[SMEM] + vmem(6),
        out_specs=tuple(vmem(4)),
        scratch_shapes=[pltpu.VMEM((channels, positions), F32)] * 4,
        compiler_params=PARAMS,
    )(pos, grad_out, query, key, value, tab_re, tab_im)

    rr3, ri3 = rr[:, None, :], ri[:, None, :]
    size = per * members
    rows = pl.BlockSpec((size, positions), lambda g: (g, 0))
    table = pl.BlockSpec((1, 32, LANES), lambda g: (g, 0, 0))
    one = pl.BlockSpec((1, 1, LANES), lambda g: (g, 0, 0))
    stat = pl.BlockSpec((1, 2, members, LANES), lambda g: (g, 0, 0, 0))
    conv, v, w, local = pl.pallas_call(
        functools.partial(local_kernel, members, modes),
        grid=(groups,),
        out_shape=(shape((channels, positions), F32), state, state, shape((groups, 4, LANES), F32)),
        in_specs=[rows, rows, table, table, one, one],
        out_specs=(rows, stat, stat, pl.BlockSpec((1, 4, LANES), lambda g: (g, 0, 0))),
        scratch_shapes=[pltpu.VMEM((8, LANES), F32), pltpu.VMEM((per, LANES), F32)],
        compiler_params=PARAMS,
        cost_estimate=pl.CostEstimate(flops=10**10, bytes_accessed=8 << 20, transcendentals=0),
    )(gate, mixed, tab_re, tab_im, rr3, ri3)
    grad_query = (grad_out.astype(F32) * conv_out.astype(F32)).astype(BF16)

    def decay(blocks):
        blocks = jnp.asarray(blocks).astype(F32) * float(positions)
        mag = jnp.exp(-rho * blocks)
        return mag * jnp.cos(angle * blocks), mag * jnp.sin(angle * blocks)

    def advance(factor, values, start, rows_):
        re, im = factor
        re = lax.dynamic_slice_in_dim(re, start, rows_, 0)[:, None, :]
        im = lax.dynamic_slice_in_dim(im, start, rows_, 0)[:, None, :]
        r, i = complex_product(re, im, values[:, 0], values[:, 1])
        return jnp.stack([r, i], axis=1)

    def half(values, which):
        n = values.shape[0] // 2
        return lax.dynamic_slice_in_dim(values, which * n, n, 0)

    halvings = []
    first = jnp.int32(0)
    level = 0
    while (1 << level) < count and level < 2:
        bit = 1 << level
        upper = (me // bit) % 2
        is_up = upper == 1
        main, side = jnp.where(is_up, x, y), jnp.where(is_up, y, x)
        n = main.shape[0] // 2
        sent = jnp.concatenate([side, half(main, 1 - upper)], axis=0)
        got = swap(sent, bit)
        full, part = got[: 2 * n], got[2 * n :]
        halvings.append((bit, upper, is_up, full, first))
        first = first + upper * n
        factor = decay(bit)
        t_main = half(main, upper) + advance(factor, half(full, upper), first, n)
        t_side = part + advance(factor, half(side, upper), first, n)
        y_next, x_next = jnp.where(is_up, t_side, t_main), jnp.where(is_up, t_main, t_side)
        own = (y, x) if level == 0 else own
        y, x = y_next, x_next
        level += 1

    n = y.shape[0]
    into_y, into_x = jnp.zeros_like(y), jnp.zeros_like(x)
    base = 1 << level
    bit = base
    while bit < count:
        upper = (me // bit) % 2
        is_up = upper == 1
        main, side = jnp.where(is_up, x, y), jnp.where(is_up, y, x)
        last = bit * 2 >= count
        got = swap(side if last else jnp.concatenate([side, main], axis=0), bit)
        got_main = got[:n]
        inside = me % bit // base
        between = jnp.where(is_up, inside, bit // base - 1 - inside) * base
        more = advance(decay(between), got_main, first, n)
        into_y = into_y + jnp.where(is_up, 0.0, more)
        into_x = into_x + jnp.where(is_up, more, 0.0)
        if not last:
            factor = decay(bit)
            t_main = main + advance(factor, got_main, first, n)
            t_side = got[n:] + advance(factor, side, first, n)
            y, x = jnp.where(is_up, t_side, t_main), jnp.where(is_up, t_main, t_side)
        bit *= 2

    for bit, upper, is_up, full, start in reversed(halvings):
        mine = jnp.stack([into_y, into_x])
        other = swap(mine, bit)
        both = jnp.concatenate(
            [jnp.where(is_up, other, mine), jnp.where(is_up, mine, other)], axis=1
        )
        in_y, in_x = both[0], both[1]
        n2 = in_y.shape[0]
        factor = decay(bit)
        into_y = jnp.where(is_up, in_y, full + advance(factor, in_y, start, n2))
        into_x = jnp.where(is_up, full + advance(factor, in_x, start, n2), in_x)

    own_y, own_x = own
    block_re, block_im = decay(1)
    total = pl.pallas_call(
        sums_kernel,
        out_shape=shape((4, groups, LANES), F32),
        in_specs=vmem(8),
        out_specs=vmem(1)[0],
        compiler_params=PARAMS,
    )(own_x, w, v, into_y, into_x, block_re, block_im, local)
    grad_key, grad_value = pl.pallas_call(
        functools.partial(finish_kernel, members, modes),
        out_shape=(shape((channels, positions), BF16), shape((channels, positions), BF16)),
        in_specs=[SMEM] + vmem(8),
        out_specs=tuple(vmem(2)),
        scratch_shapes=[pltpu.VMEM((channels, positions), F32)] * 2,
        compiler_params=PARAMS,
        cost_estimate=pl.CostEstimate(flops=10**10, bytes_accessed=8 << 20, transcendentals=0),
    )(pos, conv, into_y, tab_re, tab_im, rr3, ri3, key, value)

    bit = 1
    while bit < count:
        total = total + swap(total, bit)
        bit *= 2
    a_re, a_im, w_re, w_im = total[0], total[1], total[2], total[3]
    b_re, b_im = complex_product(rr, ri, w_re, w_im)
    plain = small[2] * a_re - small[3] * a_im
    log_rate = plain * (rho * jnp.exp(-2.0 * rho) / scale) - b_re * rho - b_im * angle
    grads = jnp.stack([log_rate, -b_im * rho, scale * a_re, -scale * a_im])
    grads = grads.reshape(4, filters, modes)
    return (grad_query, grad_key, grad_value, grads[0], grads[1], grads[2:])


def solution(mesh):
    wide = P(None, ("groups", "seq"))
    return jax.shard_map(
        body,
        mesh=mesh,
        in_specs=(wide,) * 5 + (P(),) * 4,
        out_specs=(wide, wide, wide, P("groups", None), P("groups", None), P("groups", None, None)),
        check_vma=False,
    )
```

```python
import functools

import jax
import jax.numpy as jnp
from jax import lax
from jax.experimental import pallas as pl
from jax.experimental.pallas import tpu as pltpu
from jax.sharding import PartitionSpec as P

F32 = jnp.float32
BF16 = jnp.bfloat16
LANES = 128


def complex_product(a_real, a_imag, b_real, b_imag):
    return (a_real * b_real - a_imag * b_imag, a_real * b_imag + a_imag * b_real)


def split(x):
    hi = x.astype(BF16)
    return hi, (x - hi.astype(F32)).astype(BF16)


def dot(lhs, rhs, contract):
    return lax.dot_general(lhs, rhs, (contract, ((), ())), preferred_element_type=F32)


NN = ((1,), (0,))
NT = ((1,), (1,))
TN = ((0,), (0,))


def place(per_filter, filter_ref, pos_ref):
    rows = lax.broadcasted_iota(jnp.int32, (LANES, LANES), 0)
    cols = lax.broadcasted_iota(jnp.int32, (LANES, LANES), 1)
    before = (rows < cols).astype(F32).astype(BF16)
    ones = jnp.ones((LANES, LANES), BF16)
    pair = jnp.concatenate([before, ones], axis=1)
    seen = (rows * per_filter).astype(F32)
    for block in range(filter_ref.shape[0]):
        hot = rows == filter_ref[block : block + 1, :]
        counts = dot(hot.astype(F32).astype(BF16), pair, NN)
        spot = jnp.where(hot, counts[:, :LANES] + seen, 0.0)
        pos_ref[block : block + 1, :] = jnp.sum(spot, axis=0, keepdims=True).astype(jnp.int32)
        seen = seen + counts[:, LANES:]


def three(x):
    hi = x.astype(BF16)
    rest = x - hi.astype(F32)
    mid = rest.astype(BF16)
    return hi, mid, (rest - mid.astype(F32)).astype(BF16)


def block_picks(groups, per, modes):
    filters = groups * per
    group = lax.broadcasted_iota(jnp.int32, (groups, filters), 0)
    owner = lax.broadcasted_iota(jnp.int32, (groups, filters), 1) // per
    lane = lax.broadcasted_iota(jnp.int32, (per * modes, filters), 0) // modes
    inside = lax.broadcasted_iota(jnp.int32, (per * modes, filters), 1) % per
    return (group == owner).astype(F32).astype(BF16), lane == inside


def to_groups(values, picks, per):
    pick, inside = picks
    tiled = jnp.where(inside, jnp.concatenate([values] * per, axis=0), 0.0)
    return sum(dot(pick, part, NT) for part in three(tiled))


def from_groups(values, picks, per):
    pick, inside = picks
    spread = sum(dot(part, pick, TN) for part in three(values))
    spread = jnp.where(inside, spread, 0.0)
    modes = spread.shape[0] // per
    return sum(spread[f * modes : (f + 1) * modes] for f in range(per))


def mode_rates(decay_rate, twist, length):
    rho = decay_rate / length
    return rho, twist * rho, jnp.sqrt(1.0 - jnp.exp(-2.0 * rho))


def power_of(rho, angle, steps):
    mag = jnp.exp(-rho * steps)
    return mag * jnp.cos(angle * steps), mag * jnp.sin(angle * steps)


def factor_blocks(me, count):
    blocks = [1, 2]
    bit = 4
    while bit < count:
        upper = (me // bit) % 2
        inside = me % bit // 4
        blocks += [(upper * inside + (1 - upper) * (bit // 4 - 1 - inside)) * 4, bit]
        bit *= 2
    return blocks


def setup(per, count, me, rate_ref, twist_ref, res_ref, re_ref, im_ref, factor_ref):
    modes, filters = rate_ref.shape
    length = float(LANES * count)
    picks = block_picks(filters // per, per, modes)
    rho, angle, scale = mode_rates(rate_ref[...], twist_ref[...], length)
    rho, angle, rr, ri = (
        to_groups(part, picks, per)
        for part in (rho, angle, res_ref[0] * scale, res_ref[1] * scale)
    )
    re_ref[:, 32, :], im_ref[:, 32, :] = rr, ri
    for step in [0, *range(1, 9), *range(16, 128, 8)]:
        re, im = power_of(rho, angle, float(step))
        rows = []
        if step < 8:
            rows.append(step)
        if 0 < step <= 8:
            rows.append(16 - step)
        if step % 8 == 0:
            rows.append(16 + step // 8)
        for row in rows:
            re_ref[:, row, :], im_ref[:, row, :] = re, im
    for i, blocks in enumerate(factor_blocks(me, count)):
        steps = jnp.asarray(blocks, jnp.int32).astype(F32) * float(LANES)
        factor_ref[i, 0], factor_ref[i, 1] = power_of(rho, angle, steps)


def powers(re_ref, im_ref, group, backward):
    low = slice(8, 16) if backward else slice(0, 8)
    low_re, low_im = re_ref[group, low, :], im_ref[group, low, :]
    real, imag = [], []
    for a in range(16):
        row = 16 + (15 - a if backward else a)
        high_re, high_im = re_ref[group, row : row + 1, :], im_ref[group, row : row + 1, :]
        r, i = complex_product(high_re, high_im, low_re, low_im)
        real.append(r)
        imag.append(i)
    return jnp.concatenate(real, axis=0), jnp.concatenate(imag, axis=0)


def stacked(real, imag):
    hi, lo = split(jnp.concatenate([real, imag], axis=1))
    return jnp.concatenate([hi, lo], axis=0)


def own_filter(rows, lanes, members, modes):
    row = lax.broadcasted_iota(jnp.int32, (rows, lanes), 0) // members
    lane = (lax.broadcasted_iota(jnp.int32, (rows, lanes), 1) % LANES) // modes
    return row == lane


def mode_sum(data, table, members, modes):
    out = dot(jnp.concatenate([data, data], axis=1), table, NN)
    lane = (lax.broadcasted_iota(jnp.int32, (members, 2 * LANES), 1) % LANES) // modes
    total = jnp.zeros((members, 2 * LANES), F32)
    for f in range(data.shape[0] // members):
        total = jnp.where(lane == f, out[f * members : (f + 1) * members], total)
    return total


def states_kernel(
    members, modes, count, filter_hbm, rate_hbm, twist_hbm, res_hbm,
    go_hbm, q_hbm, k_hbm, v_hbm,
    gate_ref, mixed_ref, y_lo, y_hi, x_lo, x_hi, ahead_ref, pos_ref, re_hbm, im_hbm, factor_ref,
    go_ref, k_ref, v_ref,
    filter_ref, rate_ref, twist_ref, res_ref, q_ref,
    natural_g, natural_m, grouped_g, grouped_m, re_ref, im_ref, spot_ref, sems, load_sems,
):
    channels = go_ref.shape[0]
    loads = [
        pltpu.make_async_copy(source, target, load_sems.at[i])
        for i, (source, target) in enumerate(
            (
                (filter_hbm, filter_ref), (rate_hbm, rate_ref), (twist_hbm, twist_ref),
                (res_hbm, res_ref), (go_hbm, go_ref), (q_hbm, q_ref), (k_hbm, k_ref),
                (v_hbm, v_ref),
            )
        )
    ]
    for load in loads:
        load.start()
    for load in loads[:4]:
        load.wait()
    place(members, filter_ref, pos_ref)
    spots = pltpu.make_async_copy(pos_ref, spot_ref, sems.at[0])
    spots.start()
    me = lax.axis_index("seq")
    setup(LANES // modes, count, me, rate_ref, twist_ref, res_ref, re_ref, im_ref, factor_ref)
    tables = [
        pltpu.make_async_copy(re_ref, re_hbm, sems.at[1]),
        pltpu.make_async_copy(im_ref, im_hbm, sems.at[2]),
    ]
    for table in tables:
        table.start()
    tile = 256
    for load in loads[4:]:
        load.wait()

    @pl.loop(0, channels // tile)
    def _(i):
        at = pl.ds(pl.multiple_of(i * tile, tile), tile)
        gate = (go_ref[at, :].astype(F32) * q_ref[at, :].astype(F32)).astype(BF16)
        mixed = (k_ref[at, :].astype(F32) * v_ref[at, :].astype(F32)).astype(BF16)
        natural_g[at, :] = gate.astype(F32)
        natural_m[at, :] = mixed.astype(F32)

    spots.wait()

    @pl.loop(0, channels // LANES)
    def _(i):
        base = pl.multiple_of(i * LANES, LANES)
        for u in range(LANES):
            to = spot_ref[i, u]
            grouped_g[pl.ds(to, 1), :] = natural_g[pl.ds(base + u, 1), :]
            grouped_m[pl.ds(to, 1), :] = natural_m[pl.ds(base + u, 1), :]

    size = (LANES // modes) * members
    half = y_lo.shape[0]
    upper = me % 2
    for which, (y_ref, x_ref) in enumerate(((y_lo, x_lo), (y_hi, x_hi))):

        @pl.loop(0, half, unroll=4)
        def _(i, which=which, y_ref=y_ref, x_ref=x_ref):
            g = which * half + i
            at = pl.ds(pl.multiple_of(g * size, size), size)
            gate = grouped_g[at, :].astype(BF16)
            mixed = grouped_m[at, :].astype(BF16)
            gate_ref[at, :] = gate
            mixed_ref[at, :] = mixed
            y = mode_sum(gate, stacked(*powers(re_ref, im_ref, g, False)), members, modes)
            x = mode_sum(mixed, stacked(*powers(re_ref, im_ref, g, True)), members, modes)
            y_ref[i, 0], y_ref[i, 1] = y[:, :LANES], y[:, LANES:]
            x_ref[i, 0], x_ref[i, 1] = x[:, :LANES], x[:, LANES:]

    @pl.loop(0, half)
    def _(i):
        ahead_ref[i] = jnp.where(upper == 1, y_lo[i], y_hi[i])
        ahead_ref[half + i] = jnp.where(upper == 1, x_lo[i], x_hi[i])

    for table in tables:
        table.wait()


def rates_kernel(
    members, modes, gate_ref, mixed_ref, re_ref, im_ref, v_lo, v_hi, w_lo, w_hi, ahead_ref
):
    size = (LANES // modes) * members
    half = v_lo.shape[0]
    upper = lax.axis_index("seq") % 2
    step = lax.broadcasted_iota(jnp.int32, (LANES, LANES), 0).astype(F32)
    left = float(LANES) - step
    for which, (v_ref, w_ref) in enumerate(((v_lo, w_lo), (v_hi, w_hi))):

        @pl.loop(0, half, unroll=4)
        def _(i, which=which, v_ref=v_ref, w_ref=w_ref):
            g = which * half + i
            at = pl.ds(pl.multiple_of(g * size, size), size)
            head_re, head_im = powers(re_ref, im_ref, g, False)
            back_re, back_im = powers(re_ref, im_ref, g, True)
            v = mode_sum(gate_ref[at, :], stacked(step * head_re, step * head_im), members, modes)
            w = mode_sum(mixed_ref[at, :], stacked(left * back_re, left * back_im), members, modes)
            v_ref[i, 0], v_ref[i, 1] = v[:, :LANES], v[:, LANES:]
            w_ref[i, 0], w_ref[i, 1] = w[:, :LANES], w[:, LANES:]

    @pl.loop(0, half)
    def _(i):
        ahead_ref[i] = jnp.where(upper == 1, v_lo[i], v_hi[i])
        ahead_ref[half + i] = jnp.where(upper == 1, w_lo[i], w_hi[i])


def pair(ref, i):
    return [ref[i, 0], ref[i, 1]]


def pick(flag, yes, no):
    return [jnp.where(flag, a, b) for a, b in zip(yes, no)]


def plus(a, b):
    return [p + q for p, q in zip(a, b)]


def scaled(span, a):
    return [span * p for p in a]


def place_of(level):
    me = lax.axis_index("seq")
    low, high = me % 2, (me // 2) % 2
    return (low, high, 8 * low) if level == 0 else (high, None, 8 * low + 4 * high)


def merge_kernel(level, lo1, hi1, lo2, hi2, got_ref, factor_ref, *outs):
    upper, following, base = place_of(level)
    is_up = upper == 1
    n = lo1.shape[0]
    for i in range(n):
        p = (factor_ref[level, 0, pl.ds(base + i, 1), :], factor_ref[level, 1, pl.ds(base + i, 1), :])
        y, x = pick(is_up, pair(hi1, i), pair(lo1, i)), pick(is_up, pair(hi2, i), pair(lo2, i))
        got_y, got_x = pair(got_ref, i), pair(got_ref, n + i)
        t_y = plus(pick(is_up, got_y, y), complex_product(*p, *pick(is_up, y, got_y)))
        t_x = plus(pick(is_up, x, got_x), complex_product(*p, *pick(is_up, got_x, x)))
        if level == 0:
            which, at = divmod(i, n // 2)
            for ref, t in ((outs[which], t_y), (outs[2 + which], t_x)):
                ref[at, 0], ref[at, 1] = t
        else:
            for kind, t in enumerate((t_y, t_x)):
                outs[0][kind, i, 0], outs[0][kind, i, 1] = t
    if level == 0:
        y_lo, y_hi, x_lo, x_hi, ahead = outs
        for i in range(n // 2):
            ahead[i] = jnp.where(following == 1, y_lo[i], y_hi[i])
            ahead[n // 2 + i] = jnp.where(following == 1, x_lo[i], x_hi[i])


def rows_of(pair_):
    return [jnp.sum(part, axis=0, keepdims=True) for part in pair_]


def rate_merge_kernel(
    level, y_lo, y_hi, x_lo, x_hi, got_ref, v_lo, v_hi, w_lo, w_hi, more_ref, factor_ref, *outs
):
    upper, following, base = place_of(level)
    is_up = upper == 1
    span = float(LANES << level)
    n = y_lo.shape[0]
    sums_ref = outs[-1]
    for i in range(n):
        p = (factor_ref[level, 0, pl.ds(base + i, 1), :], factor_ref[level, 1, pl.ds(base + i, 1), :])
        own = [
            pick(is_up, pair(hi, i), pair(lo, i))
            for lo, hi in ((y_lo, y_hi), (x_lo, x_hi), (v_lo, v_hi), (w_lo, w_hi))
        ]
        got = [pair(got_ref, i), pair(got_ref, n + i), pair(more_ref, i), pair(more_ref, n + i)]
        y_up, v_up = pick(is_up, own[0], got[0]), pick(is_up, own[2], got[2])
        x_low, w_low = pick(is_up, got[1], own[1]), pick(is_up, got[3], own[3])
        v_low, w_up = pick(is_up, got[2], own[2]), pick(is_up, own[3], got[3])
        t_v = plus(v_low, complex_product(*p, *plus(v_up, scaled(span, y_up))))
        t_w = plus(w_up, complex_product(*p, *plus(w_low, scaled(span, x_low))))
        a = rows_of(complex_product(*x_low, *y_up))
        w = rows_of(plus(complex_product(*w_low, *y_up), complex_product(*x_low, *v_up)))
        for kind, row in enumerate((*a, *w)):
            sums_ref[kind, i : i + 1, :] = row
        if level == 0:
            which, at = divmod(i, n // 2)
            for ref, t in ((outs[which], t_v), (outs[2 + which], t_w)):
                ref[at, 0], ref[at, 1] = t
        else:
            for kind, t in enumerate((t_v, t_w)):
                outs[0][kind, i, 0], outs[0][kind, i, 1] = t
    if level == 0:
        ahead = outs[4]
        for i in range(n // 2):
            ahead[i] = jnp.where(following == 1, outs[0][i], outs[1][i])
            ahead[n // 2 + i] = jnp.where(following == 1, outs[2][i], outs[3][i])


def total_kernel(
    calls, yx_ref, vw_ref, into_y, into_x, factor_ref, sums0_ref, sums1_ref, *refs
):
    lags, out_ref = refs[:calls], refs[-1]
    _, _, base = place_of(1)
    half = place_of(0)[2]
    span = float(LANES << 2)
    g = 0
    for lag in lags:
        for i in range(lag.shape[0]):
            for kind in range(4):
                out_ref[kind, g : g + 1, :] = lag[i, kind : kind + 1, :]
            g += 1
    for i in range(sums0_ref.shape[1]):
        for kind in range(4):
            out_ref[kind, pl.ds(half + i, 1), :] += sums0_ref[kind, i : i + 1, :]
    for i in range(into_y.shape[0]):
        p = (factor_ref[3, 0, pl.ds(base + i, 1), :], factor_ref[3, 1, pl.ds(base + i, 1), :])
        y, x = pair(into_y, i), pair(into_x, i)
        own = [(yx_ref[1, i, 0], yx_ref[1, i, 1])] + [
            (vw_ref[kind, i, 0], vw_ref[kind, i, 1]) for kind in range(2)
        ]
        a = rows_of(complex_product(*own[0], *y))
        w = rows_of(plus(complex_product(*own[2], *y), complex_product(*own[1], *x)))
        far = complex_product(*p, *rows_of(complex_product(*x, *y)))
        w = plus(w, scaled(span, far))
        for kind, row in enumerate((*a, *w)):
            out_ref[kind, pl.ds(base + i, 1), :] += row + sums1_ref[kind, i : i + 1, :]


def scan_kernel(first, last, next_last, bit, at, total_ref, got_ref, factor_ref, *refs):
    me = lax.axis_index("seq")
    is_up = (me // bit) % 2 == 1
    before, outs = (None, refs) if first else (refs[:2], refs[2:])
    _, _, base = place_of(1)
    for i in range(total_ref.shape[1]):

        def factor(which):
            return tuple(factor_ref[which, c, pl.ds(base + i, 1), :] for c in range(2))

        got_y, got_x = pair(got_ref.at[0], i), pair(got_ref.at[got_ref.shape[0] - 1], i)
        y, x = pair(total_ref.at[0], i), pair(total_ref.at[1], i)
        far_y, far_x = got_y, got_x
        if not first:
            far_y, far_x = complex_product(*factor(at), *got_y), complex_product(*factor(at), *got_x)
        none = [jnp.zeros_like(part) for part in got_y]
        into = [pick(is_up, none, far_y), pick(is_up, far_x, none)]
        for kind in range(2):
            value = into[kind] if first else plus(pair(before[kind], i), into[kind])
            outs[kind][i, 0], outs[kind][i, 1] = value
        if last:
            continue
        t_y = plus(pick(is_up, got_y, y), complex_product(*factor(at + 1), *pick(is_up, y, got_y)))
        t_x = plus(pick(is_up, x, got_x), complex_product(*factor(at + 1), *pick(is_up, got_x, x)))
        for kind, t in enumerate((t_y, t_x)):
            outs[2][kind, i, 0], outs[2][kind, i, 1] = t
        if next_last:
            outs[3][0, i, 0], outs[3][0, i, 1] = pick((me // (2 * bit)) % 2 == 1, t_y, t_x)


def down_kernel(into_ref, other_ref, got_ref, later_ref, factor_ref, out_ref):
    low, high, base = place_of(0)
    is_up = high == 1
    n = into_ref.shape[0]
    for i in range(2 * n):
        k = i % n
        mine, other = pair(into_ref, k), pair(other_ref, k)
        into = pick(is_up, other, mine) if i < n else pick(is_up, mine, other)
        own = pair(got_ref, k) if i < n else pair(later_ref, k)
        p = tuple(factor_ref[1, c, pl.ds(base + i, 1), :] for c in range(2))
        out_ref[i, 0], out_ref[i, 1] = pick(is_up, into, plus(own, complex_product(*p, *into)))


def add_kernel(a_ref, b_ref, out_ref):
    out_ref[...] = a_ref[...] + b_ref[...]


def conv_kernel(
    members, modes, gate_ref, mixed_ref, re_ref, im_ref,
    conv_ref, sums_ref, lag,
):
    per = LANES // modes
    head_re, head_im = powers(re_ref, im_ref, 0, False)
    step = lax.broadcasted_iota(jnp.int32, (LANES, LANES), 0).astype(F32)
    gate, mixed = gate_ref[...], mixed_ref[...]
    der = stacked(step * head_re, step * head_im)
    head = stacked(head_re, head_im)
    head_hi, head_lo = head[:LANES], head[LANES:]
    own8 = own_filter(per, 2 * LANES, 1, modes)
    res = jnp.concatenate([re_ref[0, 32:33, :], -im_ref[0, 32:33, :]], axis=1)
    res_hi, res_lo = split(jnp.where(own8, res, 0.0))
    filt = dot(res_hi, head_hi, NT) + dot(res_lo, head_hi, NT) + dot(res_hi, head_lo, NT)
    row = lax.broadcasted_iota(jnp.int32, (LANES, LANES), 0)
    col = lax.broadcasted_iota(jnp.int32, (LANES, LANES), 1)
    causal = col >= row
    mirror = (row + col == LANES - 1).astype(F32).astype(BF16)
    mirrored = dot(mixed, mirror, NN).astype(BF16)
    for f in range(per):
        at = slice(f * members, (f + 1) * members)
        wide = jnp.broadcast_to(filt[f : f + 1, :], (LANES, LANES))
        shifted = pltpu.roll(wide, 0, 1, stride=1, stride_axis=0)
        hi, lo = split(jnp.where(causal, shifted, 0.0))
        gate_f = gate[at]
        conv_ref[at, :] = dot(gate_f, hi, NT) + dot(gate_f, lo, NT)
        corr = jnp.where(row + col >= LANES - 1, dot(mirrored[at], gate_f, TN), 0.0)
        aligned = pltpu.roll(corr, 1, 1, stride=1, stride_axis=0)
        lag[f : f + 1, :] = jnp.sum(aligned, axis=0, keepdims=True)
    lag_hi, lag_lo = split(lag[...])
    for which, table in enumerate((head, der)):
        hi, lo = table[:LANES], table[LANES:]
        out = dot(lag_hi, hi, NN) + dot(lag_lo, hi, NN) + dot(lag_hi, lo, NN)
        out = jnp.sum(jnp.where(own8, out, 0.0), axis=0, keepdims=True)
        sums_ref[0, 2 * which : 2 * which + 1, :] = out[:, :LANES]
        sums_ref[0, 2 * which + 1 : 2 * which + 2, :] = out[:, LANES:]


def cross_kernel(
    members, modes, calls, mine_ref, other_ref, near_ref, later_ref, factor_ref, re_ref, im_ref,
    *refs,
):
    convs, out_ref = refs[:calls], refs[calls]
    per = LANES // modes
    size = per * members
    half = mine_ref.shape[0]
    is_up = lax.axis_index("seq") % 2 == 1
    lane = (lax.broadcasted_iota(jnp.int32, (members, 2 * LANES), 1) % LANES) // modes
    first = 0
    for conv_ref in convs:
        for i in range(conv_ref.shape[0] // size):
            g = first + i
            back_re, back_im = powers(re_ref, im_ref, g, True)
            rr, ri = re_ref[g, 32:33, :], im_ref[g, 32:33, :]
            coef_re, coef_im = complex_product(rr, ri, back_re, back_im)
            coef_hi, coef_lo = split(jnp.concatenate([coef_re, -coef_im], axis=1))
            k = g % half
            mine, other = pair(mine_ref, k), pair(other_ref, k)
            into = pick(is_up, other, mine) if g < half else pick(is_up, mine, other)
            own = pair(near_ref if g < half else later_ref, k)
            p = (factor_ref[0, 0, g : g + 1, :], factor_ref[0, 1, g : g + 1, :])
            yin = pick(is_up, into, plus(own, complex_product(*p, *into)))
            yin = jnp.concatenate(yin, axis=1)
            wide = jnp.concatenate([jnp.where(lane == f, yin, 0.0) for f in range(per)], axis=0)
            hi, lo = split(wide)
            total = dot(hi, coef_hi, NT) + dot(lo, coef_hi, NT) + dot(hi, coef_lo, NT)
            out_ref[g * size : (g + 1) * size, :] = conv_ref[i * size : (i + 1) * size, :] + total
        first += conv_ref.shape[0] // size


def finish_kernel(pos_ref, grouped, k_ref, v_ref, gk_hbm, gv_hbm, natural, gk_ref, gv_ref, sems):
    channels = k_ref.shape[0]
    tile = 256

    @pl.loop(0, channels // tile)
    def _(i):
        for part in range(tile // LANES):
            block = i * (tile // LANES) + part
            base = pl.multiple_of(block * LANES, LANES)
            for u in range(LANES):
                natural[pl.ds(base + u, 1), :] = grouped[pl.ds(pos_ref[block, u], 1), :]
        at = pl.ds(pl.multiple_of(i * tile, tile), tile)
        conv = natural[at, :]
        gk_ref[at, :] = (conv * v_ref[at, :].astype(F32)).astype(BF16)
        gv_ref[at, :] = (conv * k_ref[at, :].astype(F32)).astype(BF16)
        pltpu.make_async_copy(gk_ref.at[at, :], gk_hbm.at[at, :], sems.at[0]).start()
        pltpu.make_async_copy(gv_ref.at[at, :], gv_hbm.at[at, :], sems.at[1]).start()

    pltpu.make_async_copy(gk_ref, gk_hbm, sems.at[0]).wait()
    pltpu.make_async_copy(gv_ref, gv_hbm, sems.at[1]).wait()


def product_kernel(a_ref, b_hbm, out_hbm, b_ref, out_ref, sems):
    rows = a_ref.shape[0] // 4
    parts = [pl.ds(i * rows, rows) for i in range(4)]
    loads = [
        pltpu.make_async_copy(b_hbm.at[at, :], b_ref.at[at, :], sems.at[i])
        for i, at in enumerate(parts)
    ]
    for load in loads:
        load.start()
    stores = []
    for i, at in enumerate(parts):
        loads[i].wait()
        out_ref[at, :] = (a_ref[at, :].astype(F32) * b_ref[at, :].astype(F32)).astype(BF16)
        stores.append(
            pltpu.make_async_copy(out_ref.at[at, :], out_hbm.at[at, :], sems.at[4 + i])
        )
        stores[-1].start()
    for store in stores:
        store.wait()


def params_kernel(
    per, length, total_ref, last_ref, rate_ref, twist_ref, res_ref, log_rate_ref, grad_twist_ref, grad_res_ref
):
    modes, filters = rate_ref.shape
    picks = block_picks(filters // per, per, modes)
    rate, twist = rate_ref[...], twist_ref[...]
    rho, angle, scale = mode_rates(rate, twist, length)
    a_re, a_im, w_re, w_im = (
        from_groups(total_ref[i] + last_ref[i], picks, per) for i in range(4)
    )
    r0, r1 = res_ref[0], res_ref[1]
    b_re, b_im = complex_product(r0 * scale, r1 * scale, w_re, w_im)
    slope = rho * jnp.exp(-2.0 * rho) / scale
    log_rate_ref[...] = (r0 * a_re - r1 * a_im) * slope - b_re * rho - b_im * angle
    grad_twist_ref[...] = -b_im * rho
    grad_res_ref[0] = scale * a_re
    grad_res_ref[1] = -scale * a_im


def vmem(n):
    return [pl.BlockSpec(memory_space=pltpu.VMEM)] * n


SMEM = pl.BlockSpec(memory_space=pltpu.SMEM)


def params(mebibytes):
    return pltpu.CompilerParams(vmem_limit_bytes=mebibytes << 20)


def pinned(value):
    return pltpu.with_memory_space_constraint(value, pltpu.HBM)


def swap(value, bit):
    count = lax.axis_size("seq")
    return lax.ppermute(value, "seq", [(i, i ^ bit) for i in range(count)])


def lower_only(value, bit):
    count = lax.axis_size("seq")
    return lax.ppermute(value, "seq", [(i, i ^ bit) for i in range(count) if i & bit])


def together(*values):
    return lax.optimization_barrier(values)


def body(grad_out, query, key, value, conv_out, channel_filter, decay_rate, twist, residues):
    channels, positions = grad_out.shape
    filters, modes = decay_rate.shape
    members = channels // filters
    per = LANES // modes
    groups = filters // per
    count = lax.axis_size("seq")
    me = lax.axis_index("seq")
    length = positions * count
    shape = jax.ShapeDtypeStruct
    half, quarter = groups // 2, groups // 4

    def state(*lead):
        return shape((*lead, 2, members, LANES), F32)

    rates, twists = decay_rate.T, twist.T
    poles = jnp.swapaxes(residues, 1, 2)
    number = len(factor_blocks(0, count))
    hbm = pl.BlockSpec(memory_space=pltpu.HBM)
    wide = (channels, positions)
    blocks = (channels // LANES, LANES)
    table_shape = (groups, 40, LANES)
    (
        gate, mixed, y_lo, y_hi, x_lo, x_hi, ahead, pos, tab_re, tab_im, factors,
        own_out, own_key, own_value,
    ) = pl.pallas_call(
        functools.partial(states_kernel, members, modes, count),
        out_shape=(
            shape(wide, BF16), shape(wide, BF16), *[state(half)] * 4, state(groups),
            shape(blocks, jnp.int32), shape(table_shape, F32), shape(table_shape, F32),
            shape((number, 2, groups, LANES), F32), *[shape(wide, BF16)] * 3,
        ),
        in_specs=[hbm] * 8,
        out_specs=tuple(vmem(8) + [hbm] * 2 + vmem(4)),
        scratch_shapes=[
            pltpu.VMEM(blocks, jnp.int32), pltpu.VMEM((modes, filters), F32),
            pltpu.VMEM((modes, filters), F32), pltpu.VMEM((2, modes, filters), F32),
            pltpu.VMEM(wide, BF16), *[pltpu.VMEM(wide, F32)] * 4,
            *[pltpu.VMEM(table_shape, F32)] * 2, pltpu.SMEM(blocks, jnp.int32),
            pltpu.SemaphoreType.DMA((3,)), pltpu.SemaphoreType.DMA((8,)),
        ],
        compiler_params=params(20),
    )(
        *(
            pinned(part)
            for part in (
                channel_filter.reshape(blocks), rates, twists, poles,
                grad_out, query, key, value,
            )
        )
    )

    size = per * members

    def conv_call(first, number):
        rows = pl.BlockSpec((size, positions), lambda g: (g + first, 0))
        table = pl.BlockSpec((1, 40, LANES), lambda g: (g + first, 0, 0))
        return pl.pallas_call(
            functools.partial(conv_kernel, members, modes),
            grid=(number,),
            out_shape=(shape((number * size, positions), F32), shape((number, 4, LANES), F32)),
            in_specs=[rows, rows, table, table],
            out_specs=(
                pl.BlockSpec((size, positions), lambda g: (g, 0)),
                pl.BlockSpec((1, 4, LANES), lambda g: (g, 0, 0)),
            ),
            scratch_shapes=[pltpu.VMEM((per, LANES), F32)],
            compiler_params=params(8),
            cost_estimate=pl.CostEstimate(
                flops=number * 10**9, bytes_accessed=number << 19, transcendentals=0
            ),
        )(gate, mixed, tab_re, tab_im)

    def merge(level, *args):
        n = half >> level
        if level == 0:
            outs = (*[state(n // 2)] * 4, state(n))
        else:
            outs = (state(2, n),)
        return pl.pallas_call(
            functools.partial(merge_kernel, level),
            out_shape=outs,
            in_specs=vmem(6),
            out_specs=tuple(vmem(len(outs))),
            compiler_params=params(8),
        )(*args, factors)

    def rate_merge(level, *args):
        n = half >> level
        sums = shape((4, n, LANES), F32)
        if level == 0:
            outs = (*[state(n // 2)] * 4, state(n), sums)
        else:
            outs = (state(2, n), sums)
        return pl.pallas_call(
            functools.partial(rate_merge_kernel, level),
            out_shape=outs,
            in_specs=vmem(11),
            out_specs=tuple(vmem(len(outs))),
            compiler_params=params(8),
        )(*args, factors)

    got0 = swap(ahead, 1)
    ty_lo, ty_hi, tx_lo, tx_hi, ahead1 = merge(0, y_lo, y_hi, x_lo, x_hi, got0)
    ahead1, gate, mixed = together(ahead1, gate, mixed)
    got1 = swap(ahead1, 2)
    later0 = lower_only(y_hi, 1)
    vw = pl.pallas_call(
        functools.partial(rates_kernel, members, modes),
        out_shape=(*[state(half)] * 4, state(groups)),
        in_specs=vmem(4),
        out_specs=tuple(vmem(5)),
        compiler_params=params(8),
        cost_estimate=pl.CostEstimate(flops=3 * 10**9, bytes_accessed=4 << 20, transcendentals=0),
    )(gate, mixed, tab_re, tab_im)
    vw, gate, mixed = together(vw, gate, mixed)
    more0 = swap(vw[4], 1)
    parts = [4, 6, groups - 10]
    made = [conv_call(0, parts[0])]
    got1, more0, made[0] = together(got1, more0, made[0])
    (yx,) = merge(1, ty_lo, ty_hi, tx_lo, tx_hi, got1)

    base = 4
    bit, at = base, 2
    tot, sent, into = yx, yx, ()
    while bit < count:
        last, next_last = bit * 2 >= count, bit * 4 >= count
        sent, gate, mixed = together(sent, gate, mixed)
        got = swap(sent, bit)
        if bit == base:
            rate0 = rate_merge(0, y_lo, y_hi, x_lo, x_hi, got0, *vw[:4], more0)
            more1, gate, mixed = together(rate0[4], gate, mixed)
            more1 = swap(more1, 2)
            later1 = lower_only(ty_hi, 2)
        if bit == base or last:
            first = sum(parts[: len(made)])
            conv = conv_call(first, groups - first if last else parts[len(made)])
            got, conv = together(got, conv)
            made.append(conv)
        outs = [state(quarter)] * 2
        if not last:
            outs.append(state(2, quarter))
            if next_last:
                outs.append(state(1, quarter))
        outs = pl.pallas_call(
            functools.partial(scan_kernel, bit == base, last, next_last, bit, at),
            out_shape=tuple(outs),
            in_specs=vmem(3 + len(into)),
            out_specs=tuple(vmem(len(outs))),
            compiler_params=params(4),
        )(tot, got, factors, *into)
        into = outs[:2]
        if not last:
            tot, sent = outs[2], outs[-1]
        bit *= 2
        at += 2
    into_y, into_x = into
    convs, lags = zip(*made)
    calls = len(convs)
    rate1 = rate_merge(1, ty_lo, ty_hi, tx_lo, tx_hi, got1, *rate0[:4], more1)
    total = pl.pallas_call(
        functools.partial(total_kernel, calls),
        out_shape=shape((4, groups, LANES), F32),
        in_specs=vmem(7 + calls),
        out_specs=vmem(1)[0],
        compiler_params=params(8),
    )(yx, rate1[0], into_y, into_x, factors, rate0[5], rate1[1], *lags)

    def add(a, b):
        return pl.pallas_call(
            add_kernel,
            out_shape=shape((4, groups, LANES), F32),
            in_specs=vmem(2),
            out_specs=vmem(1)[0],
            compiler_params=params(2),
        )(a, b)

    other = swap(into_y, 2)
    total = add(total, swap(total, 1))
    got = swap(total, 2)
    chip = pl.pallas_call(
        down_kernel,
        out_shape=state(half),
        in_specs=vmem(5),
        out_specs=vmem(1)[0],
        compiler_params=params(4),
    )(into_y, other, got1, later1, factors)
    grad_query = pl.pallas_call(
        product_kernel,
        out_shape=shape(wide, BF16),
        in_specs=vmem(1) + [hbm],
        out_specs=hbm,
        scratch_shapes=[pltpu.VMEM(wide, BF16)] * 2 + [pltpu.SemaphoreType.DMA((8,))],
        compiler_params=params(8),
        cost_estimate=pl.CostEstimate(flops=10**9, bytes_accessed=3 << 20, transcendentals=0),
    )(own_out, pinned(conv_out))
    total = add(total, got)
    total, chip = together(total, chip)
    got = swap(total, 4)
    chip_other = swap(chip, 1)
    cost = pl.CostEstimate(flops=4 * 10**9, bytes_accessed=4 << 20, transcendentals=0)
    grouped = pl.pallas_call(
        functools.partial(cross_kernel, members, modes, calls),
        out_shape=shape(wide, F32),
        in_specs=vmem(7 + calls),
        out_specs=vmem(1)[0],
        compiler_params=params(12),
        cost_estimate=cost,
    )(chip, chip_other, got0, later0, factors, tab_re, tab_im, *convs)
    got, grouped = together(got, grouped)
    total = add(total, got)
    bit = 8
    while bit * 2 < count:
        total = add(total, swap(total, bit))
        bit *= 2
    total, grouped = together(total, grouped)
    got = swap(total, bit)
    grad_key, grad_value = pl.pallas_call(
        finish_kernel,
        out_shape=(shape(wide, BF16), shape(wide, BF16)),
        in_specs=[SMEM] + vmem(3),
        out_specs=(hbm, hbm),
        scratch_shapes=[pltpu.VMEM(wide, F32)] + [pltpu.VMEM(wide, BF16)] * 2
        + [pltpu.SemaphoreType.DMA((2,))],
        compiler_params=params(12),
        cost_estimate=cost,
    )(pos, grouped, own_key, own_value)
    got, grad_key, grad_value = together(got, grad_key, grad_value)
    one = shape((modes, filters), F32)
    log_rate, grad_twist, grad_res = pl.pallas_call(
        functools.partial(params_kernel, per, float(length)),
        out_shape=(one, one, shape((2, modes, filters), F32)),
        in_specs=vmem(5),
        out_specs=tuple(vmem(3)),
        compiler_params=params(4),
    )(total, got, rates, twists, poles)
    return (
        grad_query, grad_key, grad_value, log_rate.T, grad_twist.T, jnp.swapaxes(grad_res, 1, 2)
    )


def solution(mesh):
    wide = P(None, ("groups", "seq"))
    return jax.shard_map(
        body,
        mesh=mesh,
        in_specs=(wide,) * 5 + (P(),) * 4,
        out_specs=(wide, wide, wide, P("groups", None), P("groups", None), P("groups", None, None)),
        check_vma=False,
    )
```

```python
import functools

import jax
import jax.numpy as jnp
from jax import lax
from jax.experimental import pallas as pl
from jax.experimental.pallas import tpu as pltpu
from jax.sharding import PartitionSpec as P

F32 = jnp.float32
BF16 = jnp.bfloat16
LANES = 128
COST = 10**6
UNROLL = {4: 4, 5: 5, 6: 3}


def complex_product(a_real, a_imag, b_real, b_imag):
    return (a_real * b_real - a_imag * b_imag, a_real * b_imag + a_imag * b_real)


def split(x):
    hi = x.astype(BF16)
    return hi, (x - hi.astype(F32)).astype(BF16)


def dot(lhs, rhs, contract):
    return lax.dot_general(lhs, rhs, (contract, ((), ())), preferred_element_type=F32)


NN = ((1,), (0,))
NT = ((1,), (1,))
TN = ((0,), (0,))


def place(per_filter, filter_ref, pos_ref):
    rows = lax.broadcasted_iota(jnp.int32, (LANES, LANES), 0)
    cols = lax.broadcasted_iota(jnp.int32, (LANES, LANES), 1)
    before = (rows < cols).astype(F32).astype(BF16)
    ones = jnp.ones((LANES, LANES), BF16)
    pair = jnp.concatenate([before, ones], axis=1)
    seen = (rows * per_filter).astype(F32)
    for block in range(filter_ref.shape[0]):
        hot = rows == filter_ref[block : block + 1, :]
        counts = dot(hot.astype(F32).astype(BF16), pair, NN)
        spot = jnp.where(hot, counts[:, :LANES] + seen, 0.0)
        pos_ref[block : block + 1, :] = jnp.sum(spot, axis=0, keepdims=True).astype(jnp.int32)
        seen = seen + counts[:, LANES:]


def three(x):
    hi = x.astype(BF16)
    rest = x - hi.astype(F32)
    mid = rest.astype(BF16)
    return hi, mid, (rest - mid.astype(F32)).astype(BF16)


def block_picks(groups, per, modes):
    filters = groups * per
    group = lax.broadcasted_iota(jnp.int32, (groups, filters), 0)
    owner = lax.broadcasted_iota(jnp.int32, (groups, filters), 1) // per
    lane = lax.broadcasted_iota(jnp.int32, (per * modes, filters), 0) // modes
    inside = lax.broadcasted_iota(jnp.int32, (per * modes, filters), 1) % per
    return (group == owner).astype(F32).astype(BF16), lane == inside


def to_groups(values, picks, per):
    pick, inside = picks
    tiled = jnp.where(inside, jnp.concatenate([values] * per, axis=0), 0.0)
    return sum(dot(pick, part, NT) for part in three(tiled))


def from_groups(values, picks, per):
    pick, inside = picks
    spread = sum(dot(part, pick, TN) for part in three(values))
    spread = jnp.where(inside, spread, 0.0)
    modes = spread.shape[0] // per
    return sum(spread[f * modes : (f + 1) * modes] for f in range(per))


def mode_rates(decay_rate, twist, length):
    rho = decay_rate / length
    return rho, twist * rho, jnp.sqrt(1.0 - jnp.exp(-2.0 * rho))


def power_of(rho, angle, steps):
    mag = jnp.exp(-rho * steps)
    return mag * jnp.cos(angle * steps), mag * jnp.sin(angle * steps)


def factor_blocks(me, count):
    blocks = [1, 2]
    bit = 4
    while bit < count:
        upper = (me // bit) % 2
        inside = me % bit // 4
        blocks += [(upper * inside + (1 - upper) * (bit // 4 - 1 - inside)) * 4, bit]
        bit *= 2
    return blocks


def setup(per, count, me, rate_ref, twist_ref, res_ref, re_ref, im_ref, factor_ref):
    modes, filters = rate_ref.shape
    length = float(LANES * count)
    picks = block_picks(filters // per, per, modes)
    rho, angle, scale = mode_rates(rate_ref[...], twist_ref[...], length)
    rho, angle, rr, ri = (
        to_groups(part, picks, per)
        for part in (rho, angle, res_ref[0] * scale, res_ref[1] * scale)
    )
    re_ref[:, 32, :], im_ref[:, 32, :] = rr, ri
    known = {0: (jnp.ones_like(rho), jnp.zeros_like(rho))}
    for step in [1, 2, 4, 8, 16, 32, 64]:
        known[step] = power_of(rho, angle, float(step))
    for step in [*range(9), *range(16, 128, 8)]:
        top = 1 << max(step.bit_length() - 1, 0)
        if step not in known:
            known[step] = complex_product(*known[top], *known[step - top])
        rows = []
        if step < 8:
            rows.append(step)
        if 0 < step <= 8:
            rows.append(16 - step)
        if step % 8 == 0:
            rows.append(16 + step // 8)
        for row in rows:
            re_ref[:, row, :], im_ref[:, row, :] = known[step]
    for i, blocks in enumerate(factor_blocks(me, count)):
        steps = jnp.asarray(blocks, jnp.int32).astype(F32) * float(LANES)
        factor_ref[i, 0], factor_ref[i, 1] = power_of(rho, angle, steps)


def powers(re_ref, im_ref, group, backward):
    low = slice(8, 16) if backward else slice(0, 8)
    low_re, low_im = re_ref[group, low, :], im_ref[group, low, :]
    real, imag = [], []
    for a in range(16):
        row = 16 + (15 - a if backward else a)
        high_re, high_im = re_ref[group, row : row + 1, :], im_ref[group, row : row + 1, :]
        r, i = complex_product(high_re, high_im, low_re, low_im)
        real.append(r)
        imag.append(i)
    return jnp.concatenate(real, axis=0), jnp.concatenate(imag, axis=0)


def stacked(real, imag):
    hi, lo = split(jnp.concatenate([real, imag], axis=1))
    return jnp.concatenate([hi, lo], axis=0)


def own_filter(rows, lanes, members, modes):
    row = lax.broadcasted_iota(jnp.int32, (rows, lanes), 0) // members
    lane = (lax.broadcasted_iota(jnp.int32, (rows, lanes), 1) % LANES) // modes
    return row == lane


def mode_sum(data, table, members, modes):
    out = dot(jnp.concatenate([data, data], axis=1), table, NN)
    lane = (lax.broadcasted_iota(jnp.int32, (members, 2 * LANES), 1) % LANES) // modes
    total = jnp.zeros((members, 2 * LANES), F32)
    for f in range(data.shape[0] // members):
        total = jnp.where(lane == f, out[f * members : (f + 1) * members], total)
    return total


def states_kernel(
    members, modes, count, filter_hbm, rate_hbm, twist_hbm, res_hbm,
    go_hbm, q_hbm, k_hbm, v_hbm,
    gate_ref, mixed_ref, y_lo, y_hi, x_lo, x_hi, ahead_ref, pos_ref, re_hbm, im_hbm, factor_ref,
    go_ref, k_ref, v_ref,
    filter_ref, rate_ref, twist_ref, res_ref, q_ref,
    natural_g, natural_m, grouped_g, grouped_m, re_ref, im_ref, spot_ref, sems, load_sems,
):
    channels = go_ref.shape[0]
    loads = [
        pltpu.make_async_copy(source, target, load_sems.at[i])
        for i, (source, target) in enumerate(
            (
                (filter_hbm, filter_ref), (rate_hbm, rate_ref), (twist_hbm, twist_ref),
                (res_hbm, res_ref), (go_hbm, go_ref), (q_hbm, q_ref), (k_hbm, k_ref),
                (v_hbm, v_ref),
            )
        )
    ]
    for load in loads:
        load.start()
    for load in loads[:4]:
        load.wait()
    place(members, filter_ref, pos_ref)
    spots = pltpu.make_async_copy(pos_ref, spot_ref, sems.at[0])
    spots.start()
    me = lax.axis_index("seq")
    setup(LANES // modes, count, me, rate_ref, twist_ref, res_ref, re_ref, im_ref, factor_ref)
    tables = [
        pltpu.make_async_copy(re_ref, re_hbm, sems.at[1]),
        pltpu.make_async_copy(im_ref, im_hbm, sems.at[2]),
    ]
    for table in tables:
        table.start()
    tile = 256
    for load in loads[4:]:
        load.wait()

    @pl.loop(0, channels // tile)
    def _(i):
        at = pl.ds(pl.multiple_of(i * tile, tile), tile)
        gate = (go_ref[at, :].astype(F32) * q_ref[at, :].astype(F32)).astype(BF16)
        mixed = (k_ref[at, :].astype(F32) * v_ref[at, :].astype(F32)).astype(BF16)
        natural_g[at, :] = gate.astype(F32)
        natural_m[at, :] = mixed.astype(F32)

    spots.wait()

    @pl.loop(0, channels // LANES)
    def _(i):
        base = pl.multiple_of(i * LANES, LANES)
        for u in range(LANES):
            to = spot_ref[i, u]
            grouped_g[pl.ds(to, 1), :] = natural_g[pl.ds(base + u, 1), :]
            grouped_m[pl.ds(to, 1), :] = natural_m[pl.ds(base + u, 1), :]

    size = (LANES // modes) * members
    half = y_lo.shape[0]
    upper = me % 2
    for which, (y_ref, x_ref) in enumerate(((y_lo, x_lo), (y_hi, x_hi))):

        @pl.loop(0, half, unroll=4)
        def _(i, which=which, y_ref=y_ref, x_ref=x_ref):
            g = which * half + i
            at = pl.ds(pl.multiple_of(g * size, size), size)
            gate = grouped_g[at, :].astype(BF16)
            mixed = grouped_m[at, :].astype(BF16)
            gate_ref[at, :] = gate
            mixed_ref[at, :] = mixed
            y = mode_sum(gate, stacked(*powers(re_ref, im_ref, g, False)), members, modes)
            x = mode_sum(mixed, stacked(*powers(re_ref, im_ref, g, True)), members, modes)
            y_ref[i, 0], y_ref[i, 1] = y[:, :LANES], y[:, LANES:]
            x_ref[i, 0], x_ref[i, 1] = x[:, :LANES], x[:, LANES:]

    @pl.loop(0, half)
    def _(i):
        ahead_ref[i] = jnp.where(upper == 1, y_lo[i], y_hi[i])
        ahead_ref[half + i] = jnp.where(upper == 1, x_lo[i], x_hi[i])

    for table in tables:
        table.wait()


def rates_kernel(
    members, modes, gate_ref, mixed_ref, re_ref, im_ref, more_y, v_lo, v_hi, w_lo, w_hi, ahead_ref
):
    size = (LANES // modes) * members
    half = v_lo.shape[0]
    upper = lax.axis_index("seq") % 2
    step = lax.broadcasted_iota(jnp.int32, (LANES, LANES), 0).astype(F32)
    left = float(LANES) - step
    for which, (v_ref, w_ref) in enumerate(((v_lo, w_lo), (v_hi, w_hi))):

        @pl.loop(0, half, unroll=4)
        def _(i, which=which, v_ref=v_ref, w_ref=w_ref):
            g = which * half + i
            at = pl.ds(pl.multiple_of(g * size, size), size)
            head_re, head_im = powers(re_ref, im_ref, g, False)
            back_re, back_im = powers(re_ref, im_ref, g, True)
            v = mode_sum(gate_ref[at, :], stacked(step * head_re, step * head_im), members, modes)
            w = mode_sum(mixed_ref[at, :], stacked(left * back_re, left * back_im), members, modes)
            v_ref[i, 0], v_ref[i, 1] = v[:, :LANES], v[:, LANES:]
            w_ref[i, 0], w_ref[i, 1] = w[:, :LANES], w[:, LANES:]

    @pl.loop(0, half)
    def _(i):
        ahead_ref[i] = jnp.where(upper == 1, v_lo[i], v_hi[i])
        ahead_ref[half + i] = jnp.where(upper == 1, w_lo[i], w_hi[i])
        ahead_ref[2 * half + i] = more_y[i]


def pair(ref, i):
    return [ref[i, 0], ref[i, 1]]


def pick(flag, yes, no):
    return [jnp.where(flag, a, b) for a, b in zip(yes, no)]


def plus(a, b):
    return [p + q for p, q in zip(a, b)]


def scaled(span, a):
    return [span * p for p in a]


def place_of(level):
    me = lax.axis_index("seq")
    low, high = me % 2, (me // 2) % 2
    return (low, high, 8 * low) if level == 0 else (high, None, 8 * low + 4 * high)


def merge_kernel(level, lo1, hi1, lo2, hi2, got_ref, factor_ref, *outs):
    upper, following, base = place_of(level)
    is_up = upper == 1
    n = lo1.shape[0]
    for i in range(n):
        p = (factor_ref[level, 0, pl.ds(base + i, 1), :], factor_ref[level, 1, pl.ds(base + i, 1), :])
        y, x = pick(is_up, pair(hi1, i), pair(lo1, i)), pick(is_up, pair(hi2, i), pair(lo2, i))
        got_y, got_x = pair(got_ref, i), pair(got_ref, n + i)
        t_y = plus(pick(is_up, got_y, y), complex_product(*p, *pick(is_up, y, got_y)))
        t_x = plus(pick(is_up, x, got_x), complex_product(*p, *pick(is_up, got_x, x)))
        if level == 0:
            which, at = divmod(i, n // 2)
            for ref, t in ((outs[which], t_y), (outs[2 + which], t_x)):
                ref[at, 0], ref[at, 1] = t
        else:
            for kind, t in enumerate((t_y, t_x)):
                outs[0][kind, i, 0], outs[0][kind, i, 1] = t
    if level == 0:
        y_lo, y_hi, x_lo, x_hi, ahead = outs
        for i in range(n // 2):
            ahead[i] = jnp.where(following == 1, y_lo[i], y_hi[i])
            ahead[n // 2 + i] = jnp.where(following == 1, x_lo[i], x_hi[i])


def rows_of(pair_):
    return [jnp.sum(part, axis=0, keepdims=True) for part in pair_]


def rate_merge_kernel(
    level, y_lo, y_hi, x_lo, x_hi, got_ref, v_lo, v_hi, w_lo, w_hi, more_ref, factor_ref, *refs
):
    next_y, outs = (refs[0], refs[1:]) if level == 0 else (None, refs)
    upper, following, base = place_of(level)
    is_up = upper == 1
    span = float(LANES << level)
    n = y_lo.shape[0]
    sums_ref = outs[-1]
    for i in range(n):
        p = (factor_ref[level, 0, pl.ds(base + i, 1), :], factor_ref[level, 1, pl.ds(base + i, 1), :])
        own = [
            pick(is_up, pair(hi, i), pair(lo, i))
            for lo, hi in ((y_lo, y_hi), (x_lo, x_hi), (v_lo, v_hi), (w_lo, w_hi))
        ]
        got = [pair(got_ref, i), pair(got_ref, n + i), pair(more_ref, i), pair(more_ref, n + i)]
        y_up, v_up = pick(is_up, own[0], got[0]), pick(is_up, own[2], got[2])
        x_low, w_low = pick(is_up, got[1], own[1]), pick(is_up, got[3], own[3])
        v_low, w_up = pick(is_up, got[2], own[2]), pick(is_up, own[3], got[3])
        t_v = plus(v_low, complex_product(*p, *plus(v_up, scaled(span, y_up))))
        t_w = plus(w_up, complex_product(*p, *plus(w_low, scaled(span, x_low))))
        a = rows_of(complex_product(*x_low, *y_up))
        w = rows_of(plus(complex_product(*w_low, *y_up), complex_product(*x_low, *v_up)))
        for kind, row in enumerate((*a, *w)):
            sums_ref[kind, i : i + 1, :] = row
        if level == 0:
            which, at = divmod(i, n // 2)
            for ref, t in ((outs[which], t_v), (outs[2 + which], t_w)):
                ref[at, 0], ref[at, 1] = t
        else:
            for kind, t in enumerate((t_v, t_w)):
                outs[0][kind, i, 0], outs[0][kind, i, 1] = t
    if level == 0:
        ahead = outs[4]
        for i in range(n // 2):
            ahead[i] = jnp.where(following == 1, outs[0][i], outs[1][i])
            ahead[n // 2 + i] = jnp.where(following == 1, outs[2][i], outs[3][i])
            ahead[n + i] = next_y[i]


def total_kernel(
    calls, yx_ref, vw_ref, into_y, into_x, factor_ref, sums0_ref, sums1_ref, *refs
):
    lags, out_ref = refs[:calls], refs[-1]
    _, _, base = place_of(1)
    half = place_of(0)[2]
    span = float(LANES << 2)
    g = 0
    for lag in lags:
        for i in range(lag.shape[0]):
            for kind in range(4):
                out_ref[kind, g : g + 1, :] = lag[i, kind : kind + 1, :]
            g += 1
    for i in range(sums0_ref.shape[1]):
        for kind in range(4):
            out_ref[kind, pl.ds(half + i, 1), :] += sums0_ref[kind, i : i + 1, :]
    for i in range(into_y.shape[0]):
        p = (factor_ref[3, 0, pl.ds(base + i, 1), :], factor_ref[3, 1, pl.ds(base + i, 1), :])
        y, x = pair(into_y, i), pair(into_x, i)
        own = [(yx_ref[1, i, 0], yx_ref[1, i, 1])] + [
            (vw_ref[kind, i, 0], vw_ref[kind, i, 1]) for kind in range(2)
        ]
        a = rows_of(complex_product(*own[0], *y))
        w = rows_of(plus(complex_product(*own[2], *y), complex_product(*own[1], *x)))
        far = complex_product(*p, *rows_of(complex_product(*x, *y)))
        w = plus(w, scaled(span, far))
        for kind, row in enumerate((*a, *w)):
            out_ref[kind, pl.ds(base + i, 1), :] += row + sums1_ref[kind, i : i + 1, :]


def scan_kernel(first, last, next_last, bit, at, total_ref, got_ref, factor_ref, *refs):
    me = lax.axis_index("seq")
    is_up = (me // bit) % 2 == 1
    before, outs = (None, refs) if first else (refs[:2], refs[2:])
    _, _, base = place_of(1)
    for i in range(total_ref.shape[1]):

        def factor(which):
            return tuple(factor_ref[which, c, pl.ds(base + i, 1), :] for c in range(2))

        got_y, got_x = pair(got_ref.at[0], i), pair(got_ref.at[got_ref.shape[0] - 1], i)
        y, x = pair(total_ref.at[0], i), pair(total_ref.at[1], i)
        far_y, far_x = got_y, got_x
        if not first:
            far_y, far_x = complex_product(*factor(at), *got_y), complex_product(*factor(at), *got_x)
        none = [jnp.zeros_like(part) for part in got_y]
        into = [pick(is_up, none, far_y), pick(is_up, far_x, none)]
        for kind in range(2):
            value = into[kind] if first else plus(pair(before[kind], i), into[kind])
            outs[kind][i, 0], outs[kind][i, 1] = value
        if last:
            continue
        t_y = plus(pick(is_up, got_y, y), complex_product(*factor(at + 1), *pick(is_up, y, got_y)))
        t_x = plus(pick(is_up, x, got_x), complex_product(*factor(at + 1), *pick(is_up, got_x, x)))
        for kind, t in enumerate((t_y, t_x)):
            outs[2][kind, i, 0], outs[2][kind, i, 1] = t
        if next_last:
            outs[3][0, i, 0], outs[3][0, i, 1] = pick((me // (2 * bit)) % 2 == 1, t_y, t_x)


def down_kernel(into_ref, other_ref, got_ref, more_ref, factor_ref, out_ref):
    low, high, base = place_of(0)
    is_up = high == 1
    n = into_ref.shape[0]
    for i in range(2 * n):
        k = i % n
        mine, other = pair(into_ref, k), pair(other_ref, k)
        into = pick(is_up, other, mine) if i < n else pick(is_up, mine, other)
        own = pair(got_ref, k) if i < n else pair(more_ref, 2 * n + k)
        p = tuple(factor_ref[1, c, pl.ds(base + i, 1), :] for c in range(2))
        out_ref[i, 0], out_ref[i, 1] = pick(is_up, into, plus(own, complex_product(*p, *into)))


def add_kernel(a_ref, b_ref, out_ref):
    out_ref[...] = a_ref[...] + b_ref[...]


def conv_kernel(
    members, modes, first, unroll, gate_ref, mixed_ref, re_ref, im_ref, conv_ref, sums_ref
):
    per = LANES // modes
    size = per * members
    step = lax.broadcasted_iota(jnp.int32, (LANES, LANES), 0).astype(F32)
    own = own_filter(per, 2 * LANES, 1, modes)
    row = lax.broadcasted_iota(jnp.int32, (LANES, LANES), 0)
    col = lax.broadcasted_iota(jnp.int32, (LANES, LANES), 1)
    mirror = (row + col == LANES - 1).astype(F32).astype(BF16)
    causal, mirrored_causal = row >= col, row + col >= LANES - 1

    @pl.loop(0, conv_ref.shape[0] // size, unroll=unroll)
    def _(i):
        g = first + i
        at = pl.ds(pl.multiple_of(g * size, size), size)
        to = pl.multiple_of(i * size, size)
        gate, mixed = gate_ref[at, :], mixed_ref[at, :]
        head_re, head_im = powers(re_ref, im_ref, g, False)
        head, der = stacked(head_re, head_im), stacked(step * head_re, step * head_im)
        res = jnp.concatenate([re_ref[g, 32:33, :], -im_ref[g, 32:33, :]], axis=1)
        filt = dot(jnp.concatenate(split(jnp.where(own, res, 0.0)), axis=0), head, NT)
        filt = filt[:per, :LANES] + filt[per:, :LANES] + filt[:per, LANES:]
        filt = dot(jnp.concatenate(split(filt), axis=0), mirror, NN)
        filt = filt[:per] + filt[per:]
        turned = dot(mirror, mixed, NT).astype(BF16)
        lags = []
        for f in range(per):
            mine = slice(f * members, (f + 1) * members)
            wide = jnp.broadcast_to(filt[f : f + 1, :], (LANES, LANES))
            wide = pltpu.roll(wide, 1, 1, stride=1, stride_axis=0)
            hi, lo = split(jnp.where(causal, wide, 0.0))
            twice = jnp.concatenate([gate[mine], gate[mine]], axis=1)
            conv_ref[pl.ds(to + f * members, members), :] = dot(
                twice, jnp.concatenate([hi, lo], axis=0), NN
            )
            corr = jnp.where(mirrored_causal, dot(turned[:, mine], gate[mine], NN), 0.0)
            corr = pltpu.roll(corr, 1, 1, stride=1, stride_axis=0)
            lags.append(jnp.sum(corr, axis=0, keepdims=True))
        lag_hi, lag_lo = split(jnp.concatenate(lags, axis=0))
        lags = jnp.concatenate(
            [
                jnp.concatenate([lag_hi, lag_hi], axis=1),
                jnp.concatenate([lag_lo, jnp.zeros_like(lag_lo)], axis=1),
            ],
            axis=0,
        )
        for which, table in enumerate((head, der)):
            out = dot(lags, table, NN)
            out = jnp.where(own, out[:per] + out[per:], 0.0)
            out = jnp.sum(out, axis=0, keepdims=True)
            sums_ref[i, 2 * which : 2 * which + 1, :] = out[:, :LANES]
            sums_ref[i, 2 * which + 1 : 2 * which + 2, :] = out[:, LANES:]


def cross_kernel(
    members, modes, calls, mine_ref, other_ref, near_ref, more_ref, factor_ref, re_ref, im_ref,
    *refs,
):
    convs, out_ref = refs[:calls], refs[calls]
    per = LANES // modes
    size = per * members
    half = mine_ref.shape[0]
    is_up = lax.axis_index("seq") % 2 == 1
    lane = (lax.broadcasted_iota(jnp.int32, (members, 2 * LANES), 1) % LANES) // modes
    first = 0
    for conv_ref in convs:
        for i in range(conv_ref.shape[0] // size):
            g = first + i
            back_re, back_im = powers(re_ref, im_ref, g, True)
            rr, ri = re_ref[g, 32:33, :], im_ref[g, 32:33, :]
            coef_re, coef_im = complex_product(rr, ri, back_re, back_im)
            coef_hi, coef_lo = split(jnp.concatenate([coef_re, -coef_im], axis=1))
            k = g % half
            mine, other = pair(mine_ref, k), pair(other_ref, k)
            into = pick(is_up, other, mine) if g < half else pick(is_up, mine, other)
            own = pair(near_ref, k) if g < half else pair(more_ref, 2 * half + k)
            p = (factor_ref[0, 0, g : g + 1, :], factor_ref[0, 1, g : g + 1, :])
            yin = pick(is_up, into, plus(own, complex_product(*p, *into)))
            yin = jnp.concatenate(yin, axis=1)
            wide = jnp.concatenate([jnp.where(lane == f, yin, 0.0) for f in range(per)], axis=0)
            both = dot(
                jnp.concatenate(split(wide), axis=0),
                jnp.concatenate([coef_hi, coef_lo], axis=0),
                NT,
            )
            total = both[:size, :LANES] + both[size:, :LANES] + both[:size, LANES:]
            out_ref[g * size : (g + 1) * size, :] = conv_ref[i * size : (i + 1) * size, :] + total
        first += conv_ref.shape[0] // size


def finish_kernel(pos_ref, grouped, k_ref, v_ref, gk_hbm, gv_hbm, natural, gk_ref, gv_ref, sems):
    channels = k_ref.shape[0]
    tile = 256

    @pl.loop(0, channels // tile)
    def _(i):
        for part in range(tile // LANES):
            block = i * (tile // LANES) + part
            base = pl.multiple_of(block * LANES, LANES)
            for u in range(LANES):
                natural[pl.ds(base + u, 1), :] = grouped[pl.ds(pos_ref[block, u], 1), :]
        at = pl.ds(pl.multiple_of(i * tile, tile), tile)
        conv = natural[at, :]
        gk_ref[at, :] = (conv * v_ref[at, :].astype(F32)).astype(BF16)
        gv_ref[at, :] = (conv * k_ref[at, :].astype(F32)).astype(BF16)
        pltpu.make_async_copy(gk_ref.at[at, :], gk_hbm.at[at, :], sems.at[0]).start()
        pltpu.make_async_copy(gv_ref.at[at, :], gv_hbm.at[at, :], sems.at[1]).start()

    pltpu.make_async_copy(gk_ref, gk_hbm, sems.at[0]).wait()
    pltpu.make_async_copy(gv_ref, gv_hbm, sems.at[1]).wait()


def product_kernel(a_ref, b_hbm, out_hbm, b_ref, out_ref, sems):
    rows = a_ref.shape[0] // 4
    parts = [pl.ds(i * rows, rows) for i in range(4)]
    loads = [
        pltpu.make_async_copy(b_hbm.at[at, :], b_ref.at[at, :], sems.at[i])
        for i, at in enumerate(parts)
    ]
    for load in loads:
        load.start()
    stores = []
    for i, at in enumerate(parts):
        loads[i].wait()
        out_ref[at, :] = (a_ref[at, :].astype(F32) * b_ref[at, :].astype(F32)).astype(BF16)
        stores.append(
            pltpu.make_async_copy(out_ref.at[at, :], out_hbm.at[at, :], sems.at[4 + i])
        )
        stores[-1].start()
    for store in stores:
        store.wait()


def params_kernel(
    per, length, total_ref, last_ref, rate_ref, twist_ref, res_ref, log_rate_ref, grad_twist_ref, grad_res_ref
):
    modes, filters = rate_ref.shape
    picks = block_picks(filters // per, per, modes)
    rate, twist = rate_ref[...], twist_ref[...]
    rho, angle, scale = mode_rates(rate, twist, length)
    a_re, a_im, w_re, w_im = (
        from_groups(total_ref[i] + last_ref[i], picks, per) for i in range(4)
    )
    r0, r1 = res_ref[0], res_ref[1]
    b_re, b_im = complex_product(r0 * scale, r1 * scale, w_re, w_im)
    slope = rho * jnp.exp(-2.0 * rho) / scale
    log_rate_ref[...] = (r0 * a_re - r1 * a_im) * slope - b_re * rho - b_im * angle
    grad_twist_ref[...] = -b_im * rho
    grad_res_ref[0] = scale * a_re
    grad_res_ref[1] = -scale * a_im


def vmem(n):
    return [pl.BlockSpec(memory_space=pltpu.VMEM)] * n


SMEM = pl.BlockSpec(memory_space=pltpu.SMEM)


def params(mebibytes):
    return pltpu.CompilerParams(vmem_limit_bytes=mebibytes << 20)


def pinned(value):
    return pltpu.with_memory_space_constraint(value, pltpu.HBM)


def swap(value, bit):
    count = lax.axis_size("seq")
    return lax.ppermute(value, "seq", [(i, i ^ bit) for i in range(count)])


def together(*values):
    return lax.optimization_barrier(values)


def body(grad_out, query, key, value, conv_out, channel_filter, decay_rate, twist, residues):
    channels, positions = grad_out.shape
    filters, modes = decay_rate.shape
    members = channels // filters
    per = LANES // modes
    groups = filters // per
    count = lax.axis_size("seq")
    me = lax.axis_index("seq")
    length = positions * count
    shape = jax.ShapeDtypeStruct
    half, quarter = groups // 2, groups // 4

    def state(*lead):
        return shape((*lead, 2, members, LANES), F32)

    rates, twists = decay_rate.T, twist.T
    poles = jnp.swapaxes(residues, 1, 2)
    number = len(factor_blocks(0, count))
    hbm = pl.BlockSpec(memory_space=pltpu.HBM)
    wide = (channels, positions)
    blocks = (channels // LANES, LANES)
    table_shape = (groups, 40, LANES)
    (
        gate, mixed, y_lo, y_hi, x_lo, x_hi, ahead, pos, tab_re, tab_im, factors,
        own_out, own_key, own_value,
    ) = pl.pallas_call(
        functools.partial(states_kernel, members, modes, count),
        out_shape=(
            shape(wide, BF16), shape(wide, BF16), *[state(half)] * 4, state(groups),
            shape(blocks, jnp.int32), shape(table_shape, F32), shape(table_shape, F32),
            shape((number, 2, groups, LANES), F32), *[shape(wide, BF16)] * 3,
        ),
        in_specs=[hbm] * 8,
        out_specs=tuple(vmem(8) + [hbm] * 2 + vmem(4)),
        scratch_shapes=[
            pltpu.VMEM(blocks, jnp.int32), pltpu.VMEM((modes, filters), F32),
            pltpu.VMEM((modes, filters), F32), pltpu.VMEM((2, modes, filters), F32),
            pltpu.VMEM(wide, BF16), *[pltpu.VMEM(wide, F32)] * 4,
            *[pltpu.VMEM(table_shape, F32)] * 2, pltpu.SMEM(blocks, jnp.int32),
            pltpu.SemaphoreType.DMA((3,)), pltpu.SemaphoreType.DMA((8,)),
        ],
        compiler_params=params(20),
    )(
        *(
            pinned(part)
            for part in (
                channel_filter.reshape(blocks), rates, twists, poles,
                grad_out, query, key, value,
            )
        )
    )

    size = per * members

    def conv_call(first, number):
        return pl.pallas_call(
            functools.partial(conv_kernel, members, modes, first, UNROLL.get(number, 1)),
            out_shape=(shape((number * size, positions), F32), shape((number, 4, LANES), F32)),
            in_specs=vmem(4),
            out_specs=tuple(vmem(2)),
            compiler_params=params(8),
            cost_estimate=pl.CostEstimate(
                flops=number * COST, bytes_accessed=number << 10, transcendentals=0
            ),
        )(gate, mixed, tab_re, tab_im)

    def merge(level, *args):
        n = half >> level
        if level == 0:
            outs = (*[state(n // 2)] * 4, state(n))
        else:
            outs = (state(2, n),)
        return pl.pallas_call(
            functools.partial(merge_kernel, level),
            out_shape=outs,
            in_specs=vmem(6),
            out_specs=tuple(vmem(len(outs))),
            compiler_params=params(8),
        )(*args, factors)

    def rate_merge(level, *args):
        n = half >> level
        sums = shape((4, n, LANES), F32)
        if level == 0:
            outs = (*[state(n // 2)] * 4, state(n + n // 2), sums)
        else:
            outs = (state(2, n), sums)
        return pl.pallas_call(
            functools.partial(rate_merge_kernel, level),
            out_shape=outs,
            in_specs=vmem(len(args)),
            out_specs=tuple(vmem(len(outs))),
            compiler_params=params(8),
        )(*args)

    got0 = swap(ahead, 1)
    ty_lo, ty_hi, tx_lo, tx_hi, ahead1 = merge(0, y_lo, y_hi, x_lo, x_hi, got0)
    ahead1, gate, mixed = together(ahead1, gate, mixed)
    got1 = swap(ahead1, 2)
    vw = pl.pallas_call(
        functools.partial(rates_kernel, members, modes),
        out_shape=(*[state(half)] * 4, state(groups + half)),
        in_specs=vmem(5),
        out_specs=tuple(vmem(5)),
        compiler_params=params(8),
        cost_estimate=pl.CostEstimate(flops=2 * COST, bytes_accessed=1 << 10, transcendentals=0),
    )(gate, mixed, tab_re, tab_im, y_hi)
    parts = [5, 5, groups - 10]
    made = [conv_call(0, parts[0])]
    got1, vw, made[0] = together(got1, vw, made[0])
    more0 = swap(vw[4], 1)
    (yx,) = merge(1, ty_lo, ty_hi, tx_lo, tx_hi, got1)

    base = 4
    bit, at = base, 2
    tot, sent, into = yx, yx, ()
    while bit < count:
        last, next_last = bit * 2 >= count, bit * 4 >= count
        sent, gate, mixed = together(sent, gate, mixed)
        got = swap(sent, bit)
        if bit == base:
            rate0 = rate_merge(
                0, y_lo, y_hi, x_lo, x_hi, got0, *vw[:4], more0, factors, ty_hi
            )
            more1, gate, mixed = together(rate0[4], gate, mixed)
            more1 = swap(more1, 2)
        if bit == base or last:
            first = sum(parts[: len(made)])
            conv = conv_call(first, groups - first if last else parts[len(made)])
            got, conv = together(got, conv)
            made.append(conv)
        outs = [state(quarter)] * 2
        if not last:
            outs.append(state(2, quarter))
            if next_last:
                outs.append(state(1, quarter))
        outs = pl.pallas_call(
            functools.partial(scan_kernel, bit == base, last, next_last, bit, at),
            out_shape=tuple(outs),
            in_specs=vmem(3 + len(into)),
            out_specs=tuple(vmem(len(outs))),
            compiler_params=params(4),
        )(tot, got, factors, *into)
        into = outs[:2]
        if not last:
            tot, sent = outs[2], outs[-1]
        bit *= 2
        at += 2
    into_y, into_x = into
    convs, lags = zip(*made)
    calls = len(convs)
    rate1 = rate_merge(
        1, ty_lo, ty_hi, tx_lo, tx_hi, got1, *rate0[:4], more1, factors
    )
    total = pl.pallas_call(
        functools.partial(total_kernel, calls),
        out_shape=shape((4, groups, LANES), F32),
        in_specs=vmem(7 + calls),
        out_specs=vmem(1)[0],
        compiler_params=params(8),
    )(yx, rate1[0], into_y, into_x, factors, rate0[5], rate1[1], *lags)

    def add(a, b):
        return pl.pallas_call(
            add_kernel,
            out_shape=shape((4, groups, LANES), F32),
            in_specs=vmem(2),
            out_specs=vmem(1)[0],
            compiler_params=params(2),
        )(a, b)

    into_y, total = together(into_y, total)
    other = swap(into_y, 2)
    total = add(total, swap(total, 1))
    total, own_out = together(total, own_out)
    got = swap(total, 2)
    grad_query = pl.pallas_call(
        product_kernel,
        out_shape=shape(wide, BF16),
        in_specs=vmem(1) + [hbm],
        out_specs=hbm,
        scratch_shapes=[pltpu.VMEM(wide, BF16)] * 2 + [pltpu.SemaphoreType.DMA((8,))],
        compiler_params=params(8),
        cost_estimate=pl.CostEstimate(flops=COST, bytes_accessed=1 << 10, transcendentals=0),
    )(own_out, pinned(conv_out))
    other, grad_query = together(other, grad_query)
    chip = pl.pallas_call(
        down_kernel,
        out_shape=state(half),
        in_specs=vmem(5),
        out_specs=vmem(1)[0],
        compiler_params=params(4),
    )(into_y, other, got1, more1, factors)
    total = add(total, got)
    total, chip = together(total, chip)
    got = swap(total, 4)
    chip_other = swap(chip, 1)
    cost = pl.CostEstimate(flops=COST, bytes_accessed=1 << 10, transcendentals=0)
    grouped = pl.pallas_call(
        functools.partial(cross_kernel, members, modes, calls),
        out_shape=shape(wide, F32),
        in_specs=vmem(7 + calls),
        out_specs=vmem(1)[0],
        compiler_params=params(12),
        cost_estimate=cost,
    )(chip, chip_other, got0, more0, factors, tab_re, tab_im, *convs)
    got, grouped = together(got, grouped)
    total = add(total, got)
    bit = 8
    while bit * 2 < count:
        total = add(total, swap(total, bit))
        bit *= 2
    total, grouped = together(total, grouped)
    got = swap(total, bit)
    grad_key, grad_value = pl.pallas_call(
        finish_kernel,
        out_shape=(shape(wide, BF16), shape(wide, BF16)),
        in_specs=[SMEM] + vmem(3),
        out_specs=(hbm, hbm),
        scratch_shapes=[pltpu.VMEM(wide, F32)] + [pltpu.VMEM(wide, BF16)] * 2
        + [pltpu.SemaphoreType.DMA((2,))],
        compiler_params=params(12),
        cost_estimate=cost,
    )(pos, grouped, own_key, own_value)
    got, grad_key, grad_value = together(got, grad_key, grad_value)
    one = shape((modes, filters), F32)
    log_rate, grad_twist, grad_res = pl.pallas_call(
        functools.partial(params_kernel, per, float(length)),
        out_shape=(one, one, shape((2, modes, filters), F32)),
        in_specs=vmem(5),
        out_specs=tuple(vmem(3)),
        compiler_params=params(4),
    )(total, got, rates, twists, poles)
    return (
        grad_query, grad_key, grad_value, log_rate.T, grad_twist.T, jnp.swapaxes(grad_res, 1, 2)
    )


def solution(mesh):
    wide = P(None, ("groups", "seq"))
    return jax.shard_map(
        body,
        mesh=mesh,
        in_specs=(wide,) * 5 + (P(),) * 4,
        out_specs=(wide, wide, wide, P("groups", None), P("groups", None), P("groups", None, None)),
        check_vma=False,
    )
```

```python
import functools

import jax
import jax.numpy as jnp
from jax import lax
from jax.experimental import pallas as pl
from jax.experimental.pallas import tpu as pltpu
from jax.sharding import PartitionSpec as P

F32 = jnp.float32
BF16 = jnp.bfloat16
LANES = 128
COST = 10**6
CHUNKS = 2
BATCH = 128
UNROLL = {4: 4, 5: 5, 6: 3}


def complex_product(a_real, a_imag, b_real, b_imag):
    return (a_real * b_real - a_imag * b_imag, a_real * b_imag + a_imag * b_real)


def split(x):
    hi = x.astype(BF16)
    return hi, (x - hi.astype(F32)).astype(BF16)


def dot(lhs, rhs, contract):
    return lax.dot_general(lhs, rhs, (contract, ((), ())), preferred_element_type=F32)


NN = ((1,), (0,))
NT = ((1,), (1,))
TN = ((0,), (0,))


def place(per_filter, filter_ref, pos_ref):
    rows = lax.broadcasted_iota(jnp.int32, (LANES, LANES), 0)
    cols = lax.broadcasted_iota(jnp.int32, (LANES, LANES), 1)
    before = (rows < cols).astype(F32).astype(BF16)
    ones = jnp.ones((LANES, LANES), BF16)
    pair = jnp.concatenate([before, ones], axis=1)
    seen = (rows * per_filter).astype(F32)
    for block in range(filter_ref.shape[0]):
        hot = rows == filter_ref[block : block + 1, :]
        counts = dot(hot.astype(F32).astype(BF16), pair, NN)
        spot = jnp.where(hot, counts[:, :LANES] + seen, 0.0)
        pos_ref[block : block + 1, :] = jnp.sum(spot, axis=0, keepdims=True).astype(jnp.int32)
        seen = seen + counts[:, LANES:]


def three(x):
    hi = x.astype(BF16)
    rest = x - hi.astype(F32)
    mid = rest.astype(BF16)
    return hi, mid, (rest - mid.astype(F32)).astype(BF16)


def block_picks(groups, per, modes):
    filters = groups * per
    group = lax.broadcasted_iota(jnp.int32, (groups, filters), 0)
    owner = lax.broadcasted_iota(jnp.int32, (groups, filters), 1) // per
    lane = lax.broadcasted_iota(jnp.int32, (per * modes, filters), 0) // modes
    inside = lax.broadcasted_iota(jnp.int32, (per * modes, filters), 1) % per
    return (group == owner).astype(F32).astype(BF16), lane == inside


def to_groups(values, picks, per):
    pick, inside = picks
    tiled = jnp.where(inside, jnp.concatenate([values] * per, axis=0), 0.0)
    return sum(dot(pick, part, NT) for part in three(tiled))


def from_groups(parts, picks, per):
    pick, inside = picks
    stack = jnp.concatenate(three(jnp.concatenate(parts, axis=1)), axis=0)
    spread = dot(stack, jnp.concatenate([pick] * 3, axis=0), TN)
    lanes, outs = inside.shape[0], []
    modes = lanes // per
    for i in range(len(parts)):
        own = jnp.where(inside, spread[i * lanes : (i + 1) * lanes], 0.0)
        outs.append(sum(own[f * modes : (f + 1) * modes] for f in range(per)))
    return outs


def mode_rates(decay_rate, twist, length):
    rho = decay_rate / length
    return rho, twist * rho, jnp.sqrt(1.0 - jnp.exp(-2.0 * rho))


def power_of(rho, angle, steps):
    mag = jnp.exp(-rho * steps)
    return mag * jnp.cos(angle * steps), mag * jnp.sin(angle * steps)


def factor_blocks(me, count):
    blocks = [1, 2]
    bit = 4
    while bit < count:
        upper = (me // bit) % 2
        inside = me % bit // 4
        blocks += [(upper * inside + (1 - upper) * (bit // 4 - 1 - inside)) * 4, bit]
        bit *= 2
    return blocks


def setup(per, count, me, rate_ref, twist_ref, res_ref, re_ref, im_ref, factor_ref):
    modes, filters = rate_ref.shape
    length = float(LANES * count)
    picks = block_picks(filters // per, per, modes)
    rho, angle, scale = mode_rates(rate_ref[...], twist_ref[...], length)
    rho, angle, rr, ri = (
        to_groups(part, picks, per)
        for part in (rho, angle, res_ref[0] * scale, res_ref[1] * scale)
    )
    re_ref[:, 32, :], im_ref[:, 32, :] = rr, ri
    known = {0: (jnp.ones_like(rho), jnp.zeros_like(rho))}
    for step in [1, 2, 4, 8, 16, 32, 64]:
        known[step] = power_of(rho, angle, float(step))
    for step in [*range(9), *range(16, 128, 8)]:
        top = 1 << max(step.bit_length() - 1, 0)
        if step not in known:
            known[step] = complex_product(*known[top], *known[step - top])
        rows = []
        if step < 8:
            rows.append(step)
        if 0 < step <= 8:
            rows.append(16 - step)
        if step % 8 == 0:
            rows.append(16 + step // 8)
        for row in rows:
            re_ref[:, row, :], im_ref[:, row, :] = known[step]
    for i, blocks in enumerate(factor_blocks(me, count)):
        steps = jnp.asarray(blocks, jnp.int32).astype(F32) * float(LANES)
        factor_ref[i, 0], factor_ref[i, 1] = power_of(rho, angle, steps)


def powers(re_ref, im_ref, group, backward):
    low = slice(8, 16) if backward else slice(0, 8)
    low_re, low_im = re_ref[group, low, :], im_ref[group, low, :]
    real, imag = [], []
    for a in range(16):
        row = 16 + (15 - a if backward else a)
        high_re, high_im = re_ref[group, row : row + 1, :], im_ref[group, row : row + 1, :]
        r, i = complex_product(high_re, high_im, low_re, low_im)
        real.append(r)
        imag.append(i)
    return jnp.concatenate(real, axis=0), jnp.concatenate(imag, axis=0)


def stacked(real, imag):
    hi, lo = split(jnp.concatenate([real, imag], axis=1))
    return jnp.concatenate([hi, lo], axis=0)


def own_filter(rows, lanes, members, modes):
    row = lax.broadcasted_iota(jnp.int32, (rows, lanes), 0) // members
    lane = (lax.broadcasted_iota(jnp.int32, (rows, lanes), 1) % LANES) // modes
    return row == lane


def mode_sum(data, table, members, modes):
    out = dot(jnp.concatenate([data, data], axis=1), table, NN)
    lane = (lax.broadcasted_iota(jnp.int32, (members, 2 * LANES), 1) % LANES) // modes
    total = jnp.zeros((members, 2 * LANES), F32)
    for f in range(data.shape[0] // members):
        total = jnp.where(lane == f, out[f * members : (f + 1) * members], total)
    return total


def states_kernel(
    members, modes, count, filter_hbm, rate_hbm, twist_hbm, res_hbm,
    go_hbm, q_hbm, k_hbm, v_hbm,
    gate_ref, mixed_ref, y_lo, y_hi, x_lo, x_hi, ahead_ref, pos_ref, re_hbm, im_hbm, factor_ref,
    go_ref, k_ref, v_ref,
    filter_ref, rate_ref, twist_ref, res_ref, q_ref,
    grouped_g, grouped_m, re_ref, im_ref, spot_ref, sems, load_sems,
):
    channels = go_ref.shape[0]
    first_loads = [
        pltpu.make_async_copy(source, target, load_sems.at[i, 0])
        for i, (source, target) in enumerate(
            ((filter_hbm, filter_ref), (rate_hbm, rate_ref), (twist_hbm, twist_ref),
             (res_hbm, res_ref))
        )
    ]
    rows = channels // CHUNKS

    def loads(chunk):
        at = pl.ds(chunk * rows, rows)
        return [
            pltpu.make_async_copy(source.at[at, :], target.at[at, :], load_sems.at[i, 1 + chunk])
            for i, (source, target) in enumerate(
                ((go_hbm, go_ref), (q_hbm, q_ref), (k_hbm, k_ref), (v_hbm, v_ref))
            )
        ]

    for load in first_loads:
        load.start()
    for chunk in range(CHUNKS):
        for load in loads(chunk):
            load.start()
    for load in first_loads:
        load.wait()
    place(members, filter_ref, pos_ref)
    spots = pltpu.make_async_copy(pos_ref, spot_ref, sems.at[0])
    spots.start()
    me = lax.axis_index("seq")
    setup(LANES // modes, count, me, rate_ref, twist_ref, res_ref, re_ref, im_ref, factor_ref)
    tables = [
        pltpu.make_async_copy(re_ref, re_hbm, sems.at[1]),
        pltpu.make_async_copy(im_ref, im_hbm, sems.at[2]),
    ]
    for table in tables:
        table.start()
    spots.wait()
    for chunk in range(CHUNKS):
        for load in loads(chunk):
            load.wait()

        @pl.loop(chunk * rows // BATCH, (chunk + 1) * rows // BATCH)
        def _(i):
            base = pl.multiple_of(i * BATCH, BATCH)
            at = pl.ds(base, BATCH)
            gate = (go_ref[at, :].astype(F32) * q_ref[at, :].astype(F32)).astype(BF16)
            mixed = (k_ref[at, :].astype(F32) * v_ref[at, :].astype(F32)).astype(BF16)
            gate, mixed = gate.astype(F32), mixed.astype(F32)
            for u in range(BATCH):
                to = spot_ref[i * BATCH // LANES + u // LANES, u % LANES]
                grouped_g[pl.ds(to, 1), :] = gate[u : u + 1]
                grouped_m[pl.ds(to, 1), :] = mixed[u : u + 1]

    size = (LANES // modes) * members
    half = y_lo.shape[0]
    upper = me % 2
    for which, (y_ref, x_ref) in enumerate(((y_lo, x_lo), (y_hi, x_hi))):

        @pl.loop(0, half, unroll=4)
        def _(i, which=which, y_ref=y_ref, x_ref=x_ref):
            g = which * half + i
            at = pl.ds(pl.multiple_of(g * size, size), size)
            gate = grouped_g[at, :].astype(BF16)
            mixed = grouped_m[at, :].astype(BF16)
            gate_ref[at, :] = gate
            mixed_ref[at, :] = mixed
            y = mode_sum(gate, stacked(*powers(re_ref, im_ref, g, False)), members, modes)
            x = mode_sum(mixed, stacked(*powers(re_ref, im_ref, g, True)), members, modes)
            y_ref[i, 0], y_ref[i, 1] = y[:, :LANES], y[:, LANES:]
            x_ref[i, 0], x_ref[i, 1] = x[:, :LANES], x[:, LANES:]

    @pl.loop(0, half)
    def _(i):
        ahead_ref[i] = jnp.where(upper == 1, y_lo[i], y_hi[i])
        ahead_ref[half + i] = jnp.where(upper == 1, x_lo[i], x_hi[i])

    for table in tables:
        table.wait()


def rates_kernel(
    members, modes, gate_ref, mixed_ref, re_ref, im_ref, more_y, v_lo, v_hi, w_lo, w_hi, ahead_ref
):
    size = (LANES // modes) * members
    half = v_lo.shape[0]
    upper = lax.axis_index("seq") % 2
    step = lax.broadcasted_iota(jnp.int32, (LANES, LANES), 0).astype(F32)
    left = float(LANES) - step
    for which, (v_ref, w_ref) in enumerate(((v_lo, w_lo), (v_hi, w_hi))):

        @pl.loop(0, half, unroll=4)
        def _(i, which=which, v_ref=v_ref, w_ref=w_ref):
            g = which * half + i
            at = pl.ds(pl.multiple_of(g * size, size), size)
            head_re, head_im = powers(re_ref, im_ref, g, False)
            back_re, back_im = powers(re_ref, im_ref, g, True)
            v = mode_sum(gate_ref[at, :], stacked(step * head_re, step * head_im), members, modes)
            w = mode_sum(mixed_ref[at, :], stacked(left * back_re, left * back_im), members, modes)
            v_ref[i, 0], v_ref[i, 1] = v[:, :LANES], v[:, LANES:]
            w_ref[i, 0], w_ref[i, 1] = w[:, :LANES], w[:, LANES:]

    @pl.loop(0, half)
    def _(i):
        ahead_ref[i] = jnp.where(upper == 1, v_lo[i], v_hi[i])
        ahead_ref[half + i] = jnp.where(upper == 1, w_lo[i], w_hi[i])
        ahead_ref[2 * half + i] = more_y[i]


def pair(ref, i):
    return [ref[i, 0], ref[i, 1]]


def pick(flag, yes, no):
    return [jnp.where(flag, a, b) for a, b in zip(yes, no)]


def plus(a, b):
    return [p + q for p, q in zip(a, b)]


def scaled(span, a):
    return [span * p for p in a]


def place_of(level):
    me = lax.axis_index("seq")
    low, high = me % 2, (me // 2) % 2
    return (low, high, 8 * low) if level == 0 else (high, None, 8 * low + 4 * high)


def merge_kernel(level, lo1, hi1, lo2, hi2, got_ref, factor_ref, *outs):
    upper, following, base = place_of(level)
    is_up = upper == 1
    n = lo1.shape[0]
    for i in range(n):
        p = (factor_ref[level, 0, pl.ds(base + i, 1), :], factor_ref[level, 1, pl.ds(base + i, 1), :])
        y, x = pick(is_up, pair(hi1, i), pair(lo1, i)), pick(is_up, pair(hi2, i), pair(lo2, i))
        got_y, got_x = pair(got_ref, i), pair(got_ref, n + i)
        t_y = plus(pick(is_up, got_y, y), complex_product(*p, *pick(is_up, y, got_y)))
        t_x = plus(pick(is_up, x, got_x), complex_product(*p, *pick(is_up, got_x, x)))
        if level == 0:
            which, at = divmod(i, n // 2)
            for ref, t in ((outs[which], t_y), (outs[2 + which], t_x)):
                ref[at, 0], ref[at, 1] = t
        else:
            for kind, t in enumerate((t_y, t_x)):
                outs[0][kind, i, 0], outs[0][kind, i, 1] = t
    if level == 0:
        y_lo, y_hi, x_lo, x_hi, ahead = outs
        for i in range(n // 2):
            ahead[i] = jnp.where(following == 1, y_lo[i], y_hi[i])
            ahead[n // 2 + i] = jnp.where(following == 1, x_lo[i], x_hi[i])


def rows_of(pair_):
    return [jnp.sum(part, axis=0, keepdims=True) for part in pair_]


def rate_merge_kernel(
    level, y_lo, y_hi, x_lo, x_hi, got_ref, v_lo, v_hi, w_lo, w_hi, more_ref, factor_ref, *refs
):
    next_y, outs = (refs[0], refs[1:]) if level == 0 else (None, refs)
    upper, following, base = place_of(level)
    is_up = upper == 1
    span = float(LANES << level)
    n = y_lo.shape[0]
    sums_ref = outs[-1]
    for i in range(n):
        p = (factor_ref[level, 0, pl.ds(base + i, 1), :], factor_ref[level, 1, pl.ds(base + i, 1), :])
        own = [
            pick(is_up, pair(hi, i), pair(lo, i))
            for lo, hi in ((y_lo, y_hi), (x_lo, x_hi), (v_lo, v_hi), (w_lo, w_hi))
        ]
        got = [pair(got_ref, i), pair(got_ref, n + i), pair(more_ref, i), pair(more_ref, n + i)]
        y_up, v_up = pick(is_up, own[0], got[0]), pick(is_up, own[2], got[2])
        x_low, w_low = pick(is_up, got[1], own[1]), pick(is_up, got[3], own[3])
        v_low, w_up = pick(is_up, got[2], own[2]), pick(is_up, own[3], got[3])
        t_v = plus(v_low, complex_product(*p, *plus(v_up, scaled(span, y_up))))
        t_w = plus(w_up, complex_product(*p, *plus(w_low, scaled(span, x_low))))
        a = rows_of(complex_product(*x_low, *y_up))
        w = rows_of(plus(complex_product(*w_low, *y_up), complex_product(*x_low, *v_up)))
        for kind, row in enumerate((*a, *w)):
            sums_ref[kind, i : i + 1, :] = row
        if level == 0:
            which, at = divmod(i, n // 2)
            for ref, t in ((outs[which], t_v), (outs[2 + which], t_w)):
                ref[at, 0], ref[at, 1] = t
        else:
            for kind, t in enumerate((t_v, t_w)):
                outs[0][kind, i, 0], outs[0][kind, i, 1] = t
    if level == 0:
        ahead = outs[4]
        for i in range(n // 2):
            ahead[i] = jnp.where(following == 1, outs[0][i], outs[1][i])
            ahead[n // 2 + i] = jnp.where(following == 1, outs[2][i], outs[3][i])
            ahead[n + i] = next_y[i]


def total_kernel(
    calls, yx_ref, vw_ref, into_y, into_x, factor_ref, sums0_ref, sums1_ref, *refs
):
    lags, out_ref = refs[:calls], refs[-1]
    _, _, base = place_of(1)
    half = place_of(0)[2]
    span = float(LANES << 2)
    g = 0
    for lag in lags:
        for i in range(lag.shape[0]):
            for kind in range(4):
                out_ref[kind, g : g + 1, :] = lag[i, kind : kind + 1, :]
            g += 1
    for i in range(sums0_ref.shape[1]):
        for kind in range(4):
            out_ref[kind, pl.ds(half + i, 1), :] += sums0_ref[kind, i : i + 1, :]
    for i in range(into_y.shape[0]):
        p = (factor_ref[3, 0, pl.ds(base + i, 1), :], factor_ref[3, 1, pl.ds(base + i, 1), :])
        y, x = pair(into_y, i), pair(into_x, i)
        own = [(yx_ref[1, i, 0], yx_ref[1, i, 1])] + [
            (vw_ref[kind, i, 0], vw_ref[kind, i, 1]) for kind in range(2)
        ]
        a = rows_of(complex_product(*own[0], *y))
        w = rows_of(plus(complex_product(*own[2], *y), complex_product(*own[1], *x)))
        far = complex_product(*p, *rows_of(complex_product(*x, *y)))
        w = plus(w, scaled(span, far))
        for kind, row in enumerate((*a, *w)):
            out_ref[kind, pl.ds(base + i, 1), :] += row + sums1_ref[kind, i : i + 1, :]


def scan_kernel(first, last, next_last, bit, at, total_ref, got_ref, factor_ref, *refs):
    me = lax.axis_index("seq")
    is_up = (me // bit) % 2 == 1
    before, outs = (None, refs) if first else (refs[:2], refs[2:])
    _, _, base = place_of(1)
    for i in range(total_ref.shape[1]):

        def factor(which):
            return tuple(factor_ref[which, c, pl.ds(base + i, 1), :] for c in range(2))

        got_y, got_x = pair(got_ref.at[0], i), pair(got_ref.at[got_ref.shape[0] - 1], i)
        y, x = pair(total_ref.at[0], i), pair(total_ref.at[1], i)
        far_y, far_x = got_y, got_x
        if not first:
            far_y, far_x = complex_product(*factor(at), *got_y), complex_product(*factor(at), *got_x)
        none = [jnp.zeros_like(part) for part in got_y]
        into = [pick(is_up, none, far_y), pick(is_up, far_x, none)]
        for kind in range(2):
            value = into[kind] if first else plus(pair(before[kind], i), into[kind])
            outs[kind][i, 0], outs[kind][i, 1] = value
        if last:
            continue
        t_y = plus(pick(is_up, got_y, y), complex_product(*factor(at + 1), *pick(is_up, y, got_y)))
        t_x = plus(pick(is_up, x, got_x), complex_product(*factor(at + 1), *pick(is_up, got_x, x)))
        for kind, t in enumerate((t_y, t_x)):
            outs[2][kind, i, 0], outs[2][kind, i, 1] = t
        if next_last:
            outs[3][0, i, 0], outs[3][0, i, 1] = pick((me // (2 * bit)) % 2 == 1, t_y, t_x)


def down_kernel(into_ref, other_ref, got_ref, more_ref, factor_ref, out_ref):
    low, high, base = place_of(0)
    is_up = high == 1
    n = into_ref.shape[0]
    for i in range(2 * n):
        k = i % n
        mine, other = pair(into_ref, k), pair(other_ref, k)
        into = pick(is_up, other, mine) if i < n else pick(is_up, mine, other)
        own = pair(got_ref, k) if i < n else pair(more_ref, 2 * n + k)
        p = tuple(factor_ref[1, c, pl.ds(base + i, 1), :] for c in range(2))
        out_ref[i, 0], out_ref[i, 1] = pick(is_up, into, plus(own, complex_product(*p, *into)))


def add_kernel(a_ref, b_ref, out_ref):
    out_ref[...] = a_ref[...] + b_ref[...]


def conv_kernel(
    members, modes, first, unroll, gate_ref, mixed_ref, re_ref, im_ref, conv_ref, sums_ref
):
    per = LANES // modes
    size = per * members
    step = lax.broadcasted_iota(jnp.int32, (LANES, LANES), 0).astype(F32)
    own = own_filter(per, 2 * LANES, 1, modes)
    row = lax.broadcasted_iota(jnp.int32, (LANES, LANES), 0)
    col = lax.broadcasted_iota(jnp.int32, (LANES, LANES), 1)
    mirror = (row + col == LANES - 1).astype(F32).astype(BF16)
    causal, mirrored_causal = row >= col, row + col >= LANES - 1

    @pl.loop(0, conv_ref.shape[0] // size, unroll=unroll)
    def _(i):
        g = first + i
        at = pl.ds(pl.multiple_of(g * size, size), size)
        to = pl.multiple_of(i * size, size)
        gate, mixed = gate_ref[at, :], mixed_ref[at, :]
        head_re, head_im = powers(re_ref, im_ref, g, False)
        head, der = stacked(head_re, head_im), stacked(step * head_re, step * head_im)
        res = jnp.concatenate([re_ref[g, 32:33, :], -im_ref[g, 32:33, :]], axis=1)
        filt = dot(jnp.concatenate(split(jnp.where(own, res, 0.0)), axis=0), head, NT)
        filt = filt[:per, :LANES] + filt[per:, :LANES] + filt[:per, LANES:]
        filt = dot(jnp.concatenate(split(filt), axis=0), mirror, NN)
        filt = filt[:per] + filt[per:]
        turned = dot(mirror, mixed, NT).astype(BF16)
        lags = []
        for f in range(per):
            mine = slice(f * members, (f + 1) * members)
            wide = jnp.broadcast_to(filt[f : f + 1, :], (LANES, LANES))
            wide = pltpu.roll(wide, 1, 1, stride=1, stride_axis=0)
            hi, lo = split(jnp.where(causal, wide, 0.0))
            twice = jnp.concatenate([gate[mine], gate[mine]], axis=1)
            conv_ref[pl.ds(to + f * members, members), :] = dot(
                twice, jnp.concatenate([hi, lo], axis=0), NN
            )
            corr = jnp.where(mirrored_causal, dot(turned[:, mine], gate[mine], NN), 0.0)
            corr = pltpu.roll(corr, 1, 1, stride=1, stride_axis=0)
            lags.append(jnp.sum(corr, axis=0, keepdims=True))
        lag_hi, lag_lo = split(jnp.concatenate(lags, axis=0))
        lags = jnp.concatenate(
            [
                jnp.concatenate([lag_hi, lag_hi], axis=1),
                jnp.concatenate([lag_lo, jnp.zeros_like(lag_lo)], axis=1),
            ],
            axis=0,
        )
        for which, table in enumerate((head, der)):
            out = dot(lags, table, NN)
            out = jnp.where(own, out[:per] + out[per:], 0.0)
            out = jnp.sum(out, axis=0, keepdims=True)
            sums_ref[i, 2 * which : 2 * which + 1, :] = out[:, :LANES]
            sums_ref[i, 2 * which + 1 : 2 * which + 2, :] = out[:, LANES:]


def cross_kernel(
    members, modes, calls, mine_ref, other_ref, near_ref, more_ref, factor_ref, re_ref, im_ref,
    *refs,
):
    convs, out_ref = refs[:calls], refs[calls]
    per = LANES // modes
    size = per * members
    half = mine_ref.shape[0]
    is_up = lax.axis_index("seq") % 2 == 1
    lane = (lax.broadcasted_iota(jnp.int32, (members, 2 * LANES), 1) % LANES) // modes
    first = 0
    for conv_ref in convs:
        for i in range(conv_ref.shape[0] // size):
            g = first + i
            back_re, back_im = powers(re_ref, im_ref, g, True)
            rr, ri = re_ref[g, 32:33, :], im_ref[g, 32:33, :]
            coef_re, coef_im = complex_product(rr, ri, back_re, back_im)
            coef_hi, coef_lo = split(jnp.concatenate([coef_re, -coef_im], axis=1))
            k = g % half
            mine, other = pair(mine_ref, k), pair(other_ref, k)
            into = pick(is_up, other, mine) if g < half else pick(is_up, mine, other)
            own = pair(near_ref, k) if g < half else pair(more_ref, 2 * half + k)
            p = (factor_ref[0, 0, g : g + 1, :], factor_ref[0, 1, g : g + 1, :])
            yin = pick(is_up, into, plus(own, complex_product(*p, *into)))
            yin = jnp.concatenate(yin, axis=1)
            wide = jnp.concatenate([jnp.where(lane == f, yin, 0.0) for f in range(per)], axis=0)
            both = dot(
                jnp.concatenate(split(wide), axis=0),
                jnp.concatenate([coef_hi, coef_lo], axis=0),
                NT,
            )
            total = both[:size, :LANES] + both[size:, :LANES] + both[:size, LANES:]
            out_ref[g * size : (g + 1) * size, :] = conv_ref[i * size : (i + 1) * size, :] + total
        first += conv_ref.shape[0] // size


def finish_kernel(pos_ref, grouped, k_ref, v_ref, gk_hbm, gv_hbm, natural, gk_ref, gv_ref, sems):
    channels = k_ref.shape[0]
    tile = 256

    @pl.loop(0, channels // tile)
    def _(i):
        for part in range(tile // LANES):
            block = i * (tile // LANES) + part
            base = pl.multiple_of(block * LANES, LANES)
            for u in range(LANES):
                natural[pl.ds(base + u, 1), :] = grouped[pl.ds(pos_ref[block, u], 1), :]
        at = pl.ds(pl.multiple_of(i * tile, tile), tile)
        conv = natural[at, :]
        gk_ref[at, :] = (conv * v_ref[at, :].astype(F32)).astype(BF16)
        gv_ref[at, :] = (conv * k_ref[at, :].astype(F32)).astype(BF16)
        pltpu.make_async_copy(gk_ref.at[at, :], gk_hbm.at[at, :], sems.at[0]).start()
        pltpu.make_async_copy(gv_ref.at[at, :], gv_hbm.at[at, :], sems.at[1]).start()

    pltpu.make_async_copy(gk_ref, gk_hbm, sems.at[0]).wait()
    pltpu.make_async_copy(gv_ref, gv_hbm, sems.at[1]).wait()


def product_kernel(a_ref, b_hbm, out_hbm, b_ref, out_ref, sems):
    rows = a_ref.shape[0] // 4
    parts = [pl.ds(i * rows, rows) for i in range(4)]
    loads = [
        pltpu.make_async_copy(b_hbm.at[at, :], b_ref.at[at, :], sems.at[i])
        for i, at in enumerate(parts)
    ]
    for load in loads:
        load.start()
    stores = []
    for i, at in enumerate(parts):
        loads[i].wait()
        out_ref[at, :] = (a_ref[at, :].astype(F32) * b_ref[at, :].astype(F32)).astype(BF16)
        stores.append(
            pltpu.make_async_copy(out_ref.at[at, :], out_hbm.at[at, :], sems.at[4 + i])
        )
        stores[-1].start()
    for store in stores:
        store.wait()


def params_kernel(
    per, length, total_ref, last_ref, rate_ref, twist_ref, res_ref, log_rate_ref, grad_twist_ref, grad_res_ref
):
    modes, filters = rate_ref.shape
    picks = block_picks(filters // per, per, modes)
    rate, twist = rate_ref[...], twist_ref[...]
    rho, angle, scale = mode_rates(rate, twist, length)
    a_re, a_im, w_re, w_im = from_groups(
        [total_ref[i] + last_ref[i] for i in range(4)], picks, per
    )
    r0, r1 = res_ref[0], res_ref[1]
    b_re, b_im = complex_product(r0 * scale, r1 * scale, w_re, w_im)
    slope = rho * jnp.exp(-2.0 * rho) / scale
    log_rate_ref[...] = (r0 * a_re - r1 * a_im) * slope - b_re * rho - b_im * angle
    grad_twist_ref[...] = -b_im * rho
    grad_res_ref[0] = scale * a_re
    grad_res_ref[1] = -scale * a_im


def vmem(n):
    return [pl.BlockSpec(memory_space=pltpu.VMEM)] * n


SMEM = pl.BlockSpec(memory_space=pltpu.SMEM)


def params(mebibytes):
    return pltpu.CompilerParams(vmem_limit_bytes=mebibytes << 20)


def pinned(value):
    return pltpu.with_memory_space_constraint(value, pltpu.HBM)


def swap(value, bit):
    count = lax.axis_size("seq")
    return lax.ppermute(value, "seq", [(i, i ^ bit) for i in range(count)])


def together(*values):
    return lax.optimization_barrier(values)


def body(grad_out, query, key, value, conv_out, channel_filter, decay_rate, twist, residues):
    channels, positions = grad_out.shape
    filters, modes = decay_rate.shape
    members = channels // filters
    per = LANES // modes
    groups = filters // per
    count = lax.axis_size("seq")
    me = lax.axis_index("seq")
    length = positions * count
    shape = jax.ShapeDtypeStruct
    half, quarter = groups // 2, groups // 4

    def state(*lead):
        return shape((*lead, 2, members, LANES), F32)

    rates, twists = decay_rate.T, twist.T
    poles = jnp.swapaxes(residues, 1, 2)
    number = len(factor_blocks(0, count))
    hbm = pl.BlockSpec(memory_space=pltpu.HBM)
    wide = (channels, positions)
    blocks = (channels // LANES, LANES)
    table_shape = (groups, 40, LANES)
    (
        gate, mixed, y_lo, y_hi, x_lo, x_hi, ahead, pos, tab_re, tab_im, factors,
        own_out, own_key, own_value,
    ) = pl.pallas_call(
        functools.partial(states_kernel, members, modes, count),
        out_shape=(
            shape(wide, BF16), shape(wide, BF16), *[state(half)] * 4, state(groups),
            shape(blocks, jnp.int32), shape(table_shape, F32), shape(table_shape, F32),
            shape((number, 2, groups, LANES), F32), *[shape(wide, BF16)] * 3,
        ),
        in_specs=[hbm] * 8,
        out_specs=tuple(vmem(8) + [hbm] * 2 + vmem(4)),
        scratch_shapes=[
            pltpu.VMEM(blocks, jnp.int32), pltpu.VMEM((modes, filters), F32),
            pltpu.VMEM((modes, filters), F32), pltpu.VMEM((2, modes, filters), F32),
            pltpu.VMEM(wide, BF16), *[pltpu.VMEM(wide, F32)] * 2,
            *[pltpu.VMEM(table_shape, F32)] * 2, pltpu.SMEM(blocks, jnp.int32),
            pltpu.SemaphoreType.DMA((3,)), pltpu.SemaphoreType.DMA((4, 1 + CHUNKS)),
        ],
        compiler_params=params(20),
    )(
        *(
            pinned(part)
            for part in (
                channel_filter.reshape(blocks), rates, twists, poles,
                grad_out, query, key, value,
            )
        )
    )

    size = per * members

    def conv_call(first, number):
        return pl.pallas_call(
            functools.partial(conv_kernel, members, modes, first, UNROLL.get(number, 1)),
            out_shape=(shape((number * size, positions), F32), shape((number, 4, LANES), F32)),
            in_specs=vmem(4),
            out_specs=tuple(vmem(2)),
            compiler_params=params(8),
            cost_estimate=pl.CostEstimate(
                flops=number * COST, bytes_accessed=number << 10, transcendentals=0
            ),
        )(gate, mixed, tab_re, tab_im)

    def merge(level, *args):
        n = half >> level
        if level == 0:
            outs = (*[state(n // 2)] * 4, state(n))
        else:
            outs = (state(2, n),)
        return pl.pallas_call(
            functools.partial(merge_kernel, level),
            out_shape=outs,
            in_specs=vmem(6),
            out_specs=tuple(vmem(len(outs))),
            compiler_params=params(8),
        )(*args, factors)

    def rate_merge(level, *args):
        n = half >> level
        sums = shape((4, n, LANES), F32)
        if level == 0:
            outs = (*[state(n // 2)] * 4, state(n + n // 2), sums)
        else:
            outs = (state(2, n), sums)
        return pl.pallas_call(
            functools.partial(rate_merge_kernel, level),
            out_shape=outs,
            in_specs=vmem(len(args)),
            out_specs=tuple(vmem(len(outs))),
            compiler_params=params(8),
        )(*args)

    got0 = swap(ahead, 1)
    ty_lo, ty_hi, tx_lo, tx_hi, ahead1 = merge(0, y_lo, y_hi, x_lo, x_hi, got0)
    ahead1, gate, mixed = together(ahead1, gate, mixed)
    got1 = swap(ahead1, 2)
    vw = pl.pallas_call(
        functools.partial(rates_kernel, members, modes),
        out_shape=(*[state(half)] * 4, state(groups + half)),
        in_specs=vmem(5),
        out_specs=tuple(vmem(5)),
        compiler_params=params(8),
        cost_estimate=pl.CostEstimate(flops=2 * COST, bytes_accessed=1 << 10, transcendentals=0),
    )(gate, mixed, tab_re, tab_im, y_hi)
    parts = [5, 5, groups - 10]
    made = [conv_call(0, parts[0])]
    got1, vw, made[0] = together(got1, vw, made[0])
    more0 = swap(vw[4], 1)
    (yx,) = merge(1, ty_lo, ty_hi, tx_lo, tx_hi, got1)

    base = 4
    bit, at = base, 2
    tot, sent, into = yx, yx, ()
    while bit < count:
        last, next_last = bit * 2 >= count, bit * 4 >= count
        sent, gate, mixed = together(sent, gate, mixed)
        got = swap(sent, bit)
        if bit == base:
            rate0 = rate_merge(
                0, y_lo, y_hi, x_lo, x_hi, got0, *vw[:4], more0, factors, ty_hi
            )
            more1, gate, mixed = together(rate0[4], gate, mixed)
            more1 = swap(more1, 2)
        if bit == base or last:
            first = sum(parts[: len(made)])
            conv = conv_call(first, groups - first if last else parts[len(made)])
            got, conv = together(got, conv)
            made.append(conv)
        outs = [state(quarter)] * 2
        if not last:
            outs.append(state(2, quarter))
            if next_last:
                outs.append(state(1, quarter))
        outs = pl.pallas_call(
            functools.partial(scan_kernel, bit == base, last, next_last, bit, at),
            out_shape=tuple(outs),
            in_specs=vmem(3 + len(into)),
            out_specs=tuple(vmem(len(outs))),
            compiler_params=params(4),
        )(tot, got, factors, *into)
        into = outs[:2]
        if not last:
            tot, sent = outs[2], outs[-1]
        bit *= 2
        at += 2
    into_y, into_x = into
    convs, lags = zip(*made)
    calls = len(convs)
    rate1 = rate_merge(
        1, ty_lo, ty_hi, tx_lo, tx_hi, got1, *rate0[:4], more1, factors
    )
    total = pl.pallas_call(
        functools.partial(total_kernel, calls),
        out_shape=shape((4, groups, LANES), F32),
        in_specs=vmem(7 + calls),
        out_specs=vmem(1)[0],
        compiler_params=params(8),
    )(yx, rate1[0], into_y, into_x, factors, rate0[5], rate1[1], *lags)

    def add(a, b):
        return pl.pallas_call(
            add_kernel,
            out_shape=shape((4, groups, LANES), F32),
            in_specs=vmem(2),
            out_specs=vmem(1)[0],
            compiler_params=params(2),
        )(a, b)

    into_y, total = together(into_y, total)
    other = swap(into_y, 2)
    total = add(total, swap(total, 1))
    total, own_out = together(total, own_out)
    got = swap(total, 2)
    grad_query = pl.pallas_call(
        product_kernel,
        out_shape=shape(wide, BF16),
        in_specs=vmem(1) + [hbm],
        out_specs=hbm,
        scratch_shapes=[pltpu.VMEM(wide, BF16)] * 2 + [pltpu.SemaphoreType.DMA((8,))],
        compiler_params=params(8),
        cost_estimate=pl.CostEstimate(flops=COST, bytes_accessed=1 << 10, transcendentals=0),
    )(own_out, pinned(conv_out))
    other, grad_query = together(other, grad_query)
    chip = pl.pallas_call(
        down_kernel,
        out_shape=state(half),
        in_specs=vmem(5),
        out_specs=vmem(1)[0],
        compiler_params=params(4),
    )(into_y, other, got1, more1, factors)
    total = add(total, got)
    total, chip = together(total, chip)
    got = swap(total, 4)
    chip_other = swap(chip, 1)
    cost = pl.CostEstimate(flops=COST, bytes_accessed=1 << 10, transcendentals=0)
    grouped = pl.pallas_call(
        functools.partial(cross_kernel, members, modes, calls),
        out_shape=shape(wide, F32),
        in_specs=vmem(7 + calls),
        out_specs=vmem(1)[0],
        compiler_params=params(12),
        cost_estimate=cost,
    )(chip, chip_other, got0, more0, factors, tab_re, tab_im, *convs)
    got, grouped = together(got, grouped)
    total = add(total, got)
    bit = 8
    while bit * 2 < count:
        total = add(total, swap(total, bit))
        bit *= 2
    total, grouped = together(total, grouped)
    got = swap(total, bit)
    grad_key, grad_value = pl.pallas_call(
        finish_kernel,
        out_shape=(shape(wide, BF16), shape(wide, BF16)),
        in_specs=[SMEM] + vmem(3),
        out_specs=(hbm, hbm),
        scratch_shapes=[pltpu.VMEM(wide, F32)] + [pltpu.VMEM(wide, BF16)] * 2
        + [pltpu.SemaphoreType.DMA((2,))],
        compiler_params=params(12),
        cost_estimate=cost,
    )(pos, grouped, own_key, own_value)
    got, grad_key, grad_value = together(got, grad_key, grad_value)
    one = shape((modes, filters), F32)
    log_rate, grad_twist, grad_res = pl.pallas_call(
        functools.partial(params_kernel, per, float(length)),
        out_shape=(one, one, shape((2, modes, filters), F32)),
        in_specs=vmem(5),
        out_specs=tuple(vmem(3)),
        compiler_params=params(4),
    )(total, got, rates, twists, poles)
    return (
        grad_query, grad_key, grad_value, log_rate.T, grad_twist.T, jnp.swapaxes(grad_res, 1, 2)
    )


def solution(mesh):
    wide = P(None, ("groups", "seq"))
    return jax.shard_map(
        body,
        mesh=mesh,
        in_specs=(wide,) * 5 + (P(),) * 4,
        out_specs=(wide, wide, wide, P("groups", None), P("groups", None), P("groups", None, None)),
        check_vma=False,
    )
```

```python
import functools

import jax
import jax.numpy as jnp
from jax import lax
from jax.experimental import pallas as pl
from jax.experimental.pallas import tpu as pltpu
from jax.sharding import PartitionSpec as P

F32 = jnp.float32
BF16 = jnp.bfloat16
LANES = 128
COST = 10**6
CHUNKS = 2
BATCH = 128
UNROLL = {4: 4, 5: 5, 6: 3}


def complex_product(a_real, a_imag, b_real, b_imag):
    return (a_real * b_real - a_imag * b_imag, a_real * b_imag + a_imag * b_real)


def split(x):
    hi = x.astype(BF16)
    return hi, (x - hi.astype(F32)).astype(BF16)


def dot(lhs, rhs, contract):
    return lax.dot_general(lhs, rhs, (contract, ((), ())), preferred_element_type=F32)


NN = ((1,), (0,))
NT = ((1,), (1,))
TN = ((0,), (0,))


def place(per_filter, filter_ref, pos_ref):
    rows = lax.broadcasted_iota(jnp.int32, (LANES, LANES), 0)
    cols = lax.broadcasted_iota(jnp.int32, (LANES, LANES), 1)
    before = (rows < cols).astype(F32).astype(BF16)
    ones = jnp.ones((LANES, LANES), BF16)
    pair = jnp.concatenate([before, ones], axis=1)
    seen = (rows * per_filter).astype(F32)
    for block in range(filter_ref.shape[0]):
        hot = rows == filter_ref[block : block + 1, :]
        counts = dot(hot.astype(F32).astype(BF16), pair, NN)
        spot = jnp.where(hot, counts[:, :LANES] + seen, 0.0)
        pos_ref[block : block + 1, :] = jnp.sum(spot, axis=0, keepdims=True).astype(jnp.int32)
        seen = seen + counts[:, LANES:]


def three(x):
    hi = x.astype(BF16)
    rest = x - hi.astype(F32)
    mid = rest.astype(BF16)
    return hi, mid, (rest - mid.astype(F32)).astype(BF16)


def block_picks(groups, per, modes):
    filters = groups * per
    group = lax.broadcasted_iota(jnp.int32, (groups, filters), 0)
    owner = lax.broadcasted_iota(jnp.int32, (groups, filters), 1) // per
    lane = lax.broadcasted_iota(jnp.int32, (per * modes, filters), 0) // modes
    inside = lax.broadcasted_iota(jnp.int32, (per * modes, filters), 1) % per
    return (group == owner).astype(F32).astype(BF16), lane == inside


def to_groups(values, picks, per):
    pick, inside = picks
    tiled = jnp.where(inside, jnp.concatenate([values] * per, axis=0), 0.0)
    return sum(dot(pick, part, NT) for part in three(tiled))


def from_groups(parts, picks, per):
    pick, inside = picks
    stack = jnp.concatenate(three(jnp.concatenate(parts, axis=1)), axis=0)
    spread = dot(stack, jnp.concatenate([pick] * 3, axis=0), TN)
    lanes, outs = inside.shape[0], []
    modes = lanes // per
    for i in range(len(parts)):
        own = jnp.where(inside, spread[i * lanes : (i + 1) * lanes], 0.0)
        outs.append(sum(own[f * modes : (f + 1) * modes] for f in range(per)))
    return outs


def mode_rates(decay_rate, twist, length):
    rho = decay_rate / length
    return rho, twist * rho, jnp.sqrt(1.0 - jnp.exp(-2.0 * rho))


def power_of(rho, angle, steps):
    mag = jnp.exp(-rho * steps)
    return mag * jnp.cos(angle * steps), mag * jnp.sin(angle * steps)


def factor_blocks(me, count):
    blocks = [1, 2]
    bit = 4
    while bit < count:
        upper = (me // bit) % 2
        inside = me % bit // 4
        blocks += [(upper * inside + (1 - upper) * (bit // 4 - 1 - inside)) * 4, bit]
        bit *= 2
    return blocks


def setup(per, count, me, rate_ref, twist_ref, res_ref, re_ref, im_ref, factor_ref):
    modes, filters = rate_ref.shape
    length = float(LANES * count)
    picks = block_picks(filters // per, per, modes)
    rho, angle, scale = mode_rates(rate_ref[...], twist_ref[...], length)
    rho, angle, rr, ri = (
        to_groups(part, picks, per)
        for part in (rho, angle, res_ref[0] * scale, res_ref[1] * scale)
    )
    re_ref[:, 32, :], im_ref[:, 32, :] = rr, ri
    known = {0: (jnp.ones_like(rho), jnp.zeros_like(rho))}
    for step in [1, 2, 4, 8, 16, 32, 64]:
        known[step] = power_of(rho, angle, float(step))
    for step in [*range(9), *range(16, 128, 8)]:
        top = 1 << max(step.bit_length() - 1, 0)
        if step not in known:
            known[step] = complex_product(*known[top], *known[step - top])
        rows = []
        if step < 8:
            rows.append(step)
        if 0 < step <= 8:
            rows.append(16 - step)
        if step % 8 == 0:
            rows.append(16 + step // 8)
        for row in rows:
            re_ref[:, row, :], im_ref[:, row, :] = known[step]
    for i, blocks in enumerate(factor_blocks(me, count)):
        steps = jnp.asarray(blocks, jnp.int32).astype(F32) * float(LANES)
        factor_ref[i, 0], factor_ref[i, 1] = power_of(rho, angle, steps)


def powers(re_ref, im_ref, group, backward):
    low = slice(8, 16) if backward else slice(0, 8)
    low_re, low_im = re_ref[group, low, :], im_ref[group, low, :]
    real, imag = [], []
    for a in range(16):
        row = 16 + (15 - a if backward else a)
        high_re, high_im = re_ref[group, row : row + 1, :], im_ref[group, row : row + 1, :]
        r, i = complex_product(high_re, high_im, low_re, low_im)
        real.append(r)
        imag.append(i)
    return jnp.concatenate(real, axis=0), jnp.concatenate(imag, axis=0)


def stacked(real, imag):
    hi, lo = split(jnp.concatenate([real, imag], axis=1))
    return jnp.concatenate([hi, lo], axis=0)


def own_filter(rows, lanes, members, modes):
    row = lax.broadcasted_iota(jnp.int32, (rows, lanes), 0) // members
    lane = (lax.broadcasted_iota(jnp.int32, (rows, lanes), 1) % LANES) // modes
    return row == lane


def mode_sum(data, table, members, modes):
    out = dot(jnp.concatenate([data, data], axis=1), table, NN)
    lane = (lax.broadcasted_iota(jnp.int32, (members, 2 * LANES), 1) % LANES) // modes
    total = jnp.zeros((members, 2 * LANES), F32)
    for f in range(data.shape[0] // members):
        total = jnp.where(lane == f, out[f * members : (f + 1) * members], total)
    return total


def states_kernel(
    members, modes, count, filter_hbm, rate_hbm, twist_hbm, res_hbm,
    go_hbm, q_hbm, k_hbm, v_hbm,
    gate_ref, mixed_ref, y_lo, y_hi, x_lo, x_hi, ahead_ref, pos_ref, re_hbm, im_hbm, factor_ref,
    go_ref, k_ref, v_ref,
    filter_ref, rate_ref, twist_ref, res_ref, q_ref,
    grouped_g, grouped_m, re_ref, im_ref, spot_ref, sems, load_sems,
):
    channels = go_ref.shape[0]
    first_loads = [
        pltpu.make_async_copy(source, target, load_sems.at[i, 0])
        for i, (source, target) in enumerate(
            ((filter_hbm, filter_ref), (rate_hbm, rate_ref), (twist_hbm, twist_ref),
             (res_hbm, res_ref))
        )
    ]
    rows = channels // CHUNKS

    def loads(chunk):
        at = pl.ds(chunk * rows, rows)
        return [
            pltpu.make_async_copy(source.at[at, :], target.at[at, :], load_sems.at[i, 1 + chunk])
            for i, (source, target) in enumerate(
                ((go_hbm, go_ref), (q_hbm, q_ref), (k_hbm, k_ref), (v_hbm, v_ref))
            )
        ]

    for load in first_loads:
        load.start()
    for chunk in range(CHUNKS):
        for load in loads(chunk):
            load.start()
    for load in first_loads:
        load.wait()
    place(members, filter_ref, pos_ref)
    spots = pltpu.make_async_copy(pos_ref, spot_ref, sems.at[0])
    spots.start()
    me = lax.axis_index("seq")
    setup(LANES // modes, count, me, rate_ref, twist_ref, res_ref, re_ref, im_ref, factor_ref)
    tables = [
        pltpu.make_async_copy(re_ref, re_hbm, sems.at[1]),
        pltpu.make_async_copy(im_ref, im_hbm, sems.at[2]),
    ]
    for table in tables:
        table.start()
    spots.wait()
    for chunk in range(CHUNKS):
        for load in loads(chunk):
            load.wait()

        @pl.loop(chunk * rows // BATCH, (chunk + 1) * rows // BATCH)
        def _(i):
            base = pl.multiple_of(i * BATCH, BATCH)
            at = pl.ds(base, BATCH)
            gate = (go_ref[at, :].astype(F32) * q_ref[at, :].astype(F32)).astype(BF16)
            mixed = (k_ref[at, :].astype(F32) * v_ref[at, :].astype(F32)).astype(BF16)
            gate, mixed = gate.astype(F32), mixed.astype(F32)
            for u in range(BATCH):
                to = spot_ref[i * BATCH // LANES + u // LANES, u % LANES]
                grouped_g[pl.ds(to, 1), :] = gate[u : u + 1]
                grouped_m[pl.ds(to, 1), :] = mixed[u : u + 1]

    size = (LANES // modes) * members
    half = y_lo.shape[0]
    upper = me % 2
    for which, (y_ref, x_ref) in enumerate(((y_lo, x_lo), (y_hi, x_hi))):

        @pl.loop(0, half, unroll=8)
        def _(i, which=which, y_ref=y_ref, x_ref=x_ref):
            g = which * half + i
            at = pl.ds(pl.multiple_of(g * size, size), size)
            gate = grouped_g[at, :].astype(BF16)
            mixed = grouped_m[at, :].astype(BF16)
            gate_ref[at, :] = gate
            mixed_ref[at, :] = mixed
            y = mode_sum(gate, stacked(*powers(re_ref, im_ref, g, False)), members, modes)
            x = mode_sum(mixed, stacked(*powers(re_ref, im_ref, g, True)), members, modes)
            y_ref[i, 0], y_ref[i, 1] = y[:, :LANES], y[:, LANES:]
            x_ref[i, 0], x_ref[i, 1] = x[:, :LANES], x[:, LANES:]

    @pl.loop(0, half)
    def _(i):
        ahead_ref[i] = jnp.where(upper == 1, y_lo[i], y_hi[i])
        ahead_ref[half + i] = jnp.where(upper == 1, x_lo[i], x_hi[i])

    for table in tables:
        table.wait()


def rates_kernel(
    members, modes, gate_ref, mixed_ref, re_ref, im_ref, more_y, v_lo, v_hi, w_lo, w_hi, ahead_ref
):
    size = (LANES // modes) * members
    half = v_lo.shape[0]
    upper = lax.axis_index("seq") % 2
    step = lax.broadcasted_iota(jnp.int32, (LANES, LANES), 0).astype(F32)
    left = float(LANES) - step
    for which, (v_ref, w_ref) in enumerate(((v_lo, w_lo), (v_hi, w_hi))):

        @pl.loop(0, half, unroll=4)
        def _(i, which=which, v_ref=v_ref, w_ref=w_ref):
            g = which * half + i
            at = pl.ds(pl.multiple_of(g * size, size), size)
            head_re, head_im = powers(re_ref, im_ref, g, False)
            back_re, back_im = powers(re_ref, im_ref, g, True)
            v = mode_sum(gate_ref[at, :], stacked(step * head_re, step * head_im), members, modes)
            w = mode_sum(mixed_ref[at, :], stacked(left * back_re, left * back_im), members, modes)
            v_ref[i, 0], v_ref[i, 1] = v[:, :LANES], v[:, LANES:]
            w_ref[i, 0], w_ref[i, 1] = w[:, :LANES], w[:, LANES:]

    @pl.loop(0, half)
    def _(i):
        ahead_ref[i] = jnp.where(upper == 1, v_lo[i], v_hi[i])
        ahead_ref[half + i] = jnp.where(upper == 1, w_lo[i], w_hi[i])
        ahead_ref[2 * half + i] = more_y[i]


def pair(ref, i):
    return [ref[i, 0], ref[i, 1]]


def pick(flag, yes, no):
    return [jnp.where(flag, a, b) for a, b in zip(yes, no)]


def plus(a, b):
    return [p + q for p, q in zip(a, b)]


def scaled(span, a):
    return [span * p for p in a]


def place_of(level):
    me = lax.axis_index("seq")
    low, high = me % 2, (me // 2) % 2
    return (low, high, 8 * low) if level == 0 else (high, None, 8 * low + 4 * high)


def merge_kernel(level, lo1, hi1, lo2, hi2, got_ref, factor_ref, *outs):
    upper, following, base = place_of(level)
    is_up = upper == 1
    n = lo1.shape[0]
    for i in range(n):
        p = (factor_ref[level, 0, pl.ds(base + i, 1), :], factor_ref[level, 1, pl.ds(base + i, 1), :])
        y, x = pick(is_up, pair(hi1, i), pair(lo1, i)), pick(is_up, pair(hi2, i), pair(lo2, i))
        got_y, got_x = pair(got_ref, i), pair(got_ref, n + i)
        t_y = plus(pick(is_up, got_y, y), complex_product(*p, *pick(is_up, y, got_y)))
        t_x = plus(pick(is_up, x, got_x), complex_product(*p, *pick(is_up, got_x, x)))
        if level == 0:
            which, at = divmod(i, n // 2)
            for ref, t in ((outs[which], t_y), (outs[2 + which], t_x)):
                ref[at, 0], ref[at, 1] = t
        else:
            for kind, t in enumerate((t_y, t_x)):
                outs[0][kind, i, 0], outs[0][kind, i, 1] = t
    if level == 0:
        y_lo, y_hi, x_lo, x_hi, ahead = outs
        for i in range(n // 2):
            ahead[i] = jnp.where(following == 1, y_lo[i], y_hi[i])
            ahead[n // 2 + i] = jnp.where(following == 1, x_lo[i], x_hi[i])


def rows_of(pair_):
    return [jnp.sum(part, axis=0, keepdims=True) for part in pair_]


def rate_merge_kernel(
    level, y_lo, y_hi, x_lo, x_hi, got_ref, v_lo, v_hi, w_lo, w_hi, more_ref, factor_ref, *refs
):
    next_y, outs = (refs[0], refs[1:]) if level == 0 else (None, refs)
    upper, following, base = place_of(level)
    is_up = upper == 1
    span = float(LANES << level)
    n = y_lo.shape[0]
    sums_ref = outs[-1]
    for i in range(n):
        p = (factor_ref[level, 0, pl.ds(base + i, 1), :], factor_ref[level, 1, pl.ds(base + i, 1), :])
        own = [
            pick(is_up, pair(hi, i), pair(lo, i))
            for lo, hi in ((y_lo, y_hi), (x_lo, x_hi), (v_lo, v_hi), (w_lo, w_hi))
        ]
        got = [pair(got_ref, i), pair(got_ref, n + i), pair(more_ref, i), pair(more_ref, n + i)]
        y_up, v_up = pick(is_up, own[0], got[0]), pick(is_up, own[2], got[2])
        x_low, w_low = pick(is_up, got[1], own[1]), pick(is_up, got[3], own[3])
        v_low, w_up = pick(is_up, got[2], own[2]), pick(is_up, own[3], got[3])
        t_v = plus(v_low, complex_product(*p, *plus(v_up, scaled(span, y_up))))
        t_w = plus(w_up, complex_product(*p, *plus(w_low, scaled(span, x_low))))
        a = rows_of(complex_product(*x_low, *y_up))
        w = rows_of(plus(complex_product(*w_low, *y_up), complex_product(*x_low, *v_up)))
        for kind, row in enumerate((*a, *w)):
            sums_ref[kind, i : i + 1, :] = row
        if level == 0:
            which, at = divmod(i, n // 2)
            for ref, t in ((outs[which], t_v), (outs[2 + which], t_w)):
                ref[at, 0], ref[at, 1] = t
        else:
            for kind, t in enumerate((t_v, t_w)):
                outs[0][kind, i, 0], outs[0][kind, i, 1] = t
    if level == 0:
        ahead = outs[4]
        for i in range(n // 2):
            ahead[i] = jnp.where(following == 1, outs[0][i], outs[1][i])
            ahead[n // 2 + i] = jnp.where(following == 1, outs[2][i], outs[3][i])
            ahead[n + i] = next_y[i]


def total_kernel(
    calls, yx_ref, vw_ref, into_y, into_x, factor_ref, sums0_ref, sums1_ref, *refs
):
    lags, out_ref = refs[:calls], refs[-1]
    _, _, base = place_of(1)
    half = place_of(0)[2]
    span = float(LANES << 2)
    g = 0
    for lag in lags:
        for i in range(lag.shape[0]):
            for kind in range(4):
                out_ref[kind, g : g + 1, :] = lag[i, kind : kind + 1, :]
            g += 1
    for i in range(sums0_ref.shape[1]):
        for kind in range(4):
            out_ref[kind, pl.ds(half + i, 1), :] += sums0_ref[kind, i : i + 1, :]
    for i in range(into_y.shape[0]):
        p = (factor_ref[3, 0, pl.ds(base + i, 1), :], factor_ref[3, 1, pl.ds(base + i, 1), :])
        y, x = pair(into_y, i), pair(into_x, i)
        own = [(yx_ref[1, i, 0], yx_ref[1, i, 1])] + [
            (vw_ref[kind, i, 0], vw_ref[kind, i, 1]) for kind in range(2)
        ]
        a = rows_of(complex_product(*own[0], *y))
        w = rows_of(plus(complex_product(*own[2], *y), complex_product(*own[1], *x)))
        far = complex_product(*p, *rows_of(complex_product(*x, *y)))
        w = plus(w, scaled(span, far))
        for kind, row in enumerate((*a, *w)):
            out_ref[kind, pl.ds(base + i, 1), :] += row + sums1_ref[kind, i : i + 1, :]


def scan_kernel(first, last, next_last, bit, at, total_ref, got_ref, factor_ref, *refs):
    me = lax.axis_index("seq")
    is_up = (me // bit) % 2 == 1
    before, outs = (None, refs) if first else (refs[:2], refs[2:])
    _, _, base = place_of(1)
    for i in range(total_ref.shape[1]):

        def factor(which):
            return tuple(factor_ref[which, c, pl.ds(base + i, 1), :] for c in range(2))

        got_y, got_x = pair(got_ref.at[0], i), pair(got_ref.at[got_ref.shape[0] - 1], i)
        y, x = pair(total_ref.at[0], i), pair(total_ref.at[1], i)
        far_y, far_x = got_y, got_x
        if not first:
            far_y, far_x = complex_product(*factor(at), *got_y), complex_product(*factor(at), *got_x)
        none = [jnp.zeros_like(part) for part in got_y]
        into = [pick(is_up, none, far_y), pick(is_up, far_x, none)]
        for kind in range(2):
            value = into[kind] if first else plus(pair(before[kind], i), into[kind])
            outs[kind][i, 0], outs[kind][i, 1] = value
        if last:
            continue
        t_y = plus(pick(is_up, got_y, y), complex_product(*factor(at + 1), *pick(is_up, y, got_y)))
        t_x = plus(pick(is_up, x, got_x), complex_product(*factor(at + 1), *pick(is_up, got_x, x)))
        for kind, t in enumerate((t_y, t_x)):
            outs[2][kind, i, 0], outs[2][kind, i, 1] = t
        if next_last:
            outs[3][0, i, 0], outs[3][0, i, 1] = pick((me // (2 * bit)) % 2 == 1, t_y, t_x)


def down_kernel(into_ref, other_ref, got_ref, more_ref, factor_ref, out_ref):
    low, high, base = place_of(0)
    is_up = high == 1
    n = into_ref.shape[0]
    for i in range(2 * n):
        k = i % n
        mine, other = pair(into_ref, k), pair(other_ref, k)
        into = pick(is_up, other, mine) if i < n else pick(is_up, mine, other)
        own = pair(got_ref, k) if i < n else pair(more_ref, 2 * n + k)
        p = tuple(factor_ref[1, c, pl.ds(base + i, 1), :] for c in range(2))
        out_ref[i, 0], out_ref[i, 1] = pick(is_up, into, plus(own, complex_product(*p, *into)))


def add_kernel(a_ref, b_ref, out_ref):
    out_ref[...] = a_ref[...] + b_ref[...]


def conv_kernel(
    members, modes, first, unroll, gate_ref, mixed_ref, re_ref, im_ref, conv_ref, sums_ref
):
    per = LANES // modes
    size = per * members
    step = lax.broadcasted_iota(jnp.int32, (LANES, LANES), 0).astype(F32)
    own = own_filter(per, 2 * LANES, 1, modes)
    row = lax.broadcasted_iota(jnp.int32, (LANES, LANES), 0)
    col = lax.broadcasted_iota(jnp.int32, (LANES, LANES), 1)
    mirror = (row + col == LANES - 1).astype(F32).astype(BF16)
    causal, mirrored_causal = row >= col, row + col >= LANES - 1

    @pl.loop(0, conv_ref.shape[0] // size, unroll=unroll)
    def _(i):
        g = first + i
        at = pl.ds(pl.multiple_of(g * size, size), size)
        to = pl.multiple_of(i * size, size)
        gate, mixed = gate_ref[at, :], mixed_ref[at, :]
        head_re, head_im = powers(re_ref, im_ref, g, False)
        head, der = stacked(head_re, head_im), stacked(step * head_re, step * head_im)
        res = jnp.concatenate([re_ref[g, 32:33, :], -im_ref[g, 32:33, :]], axis=1)
        filt = dot(jnp.concatenate(split(jnp.where(own, res, 0.0)), axis=0), head, NT)
        filt = filt[:per, :LANES] + filt[per:, :LANES] + filt[:per, LANES:]
        filt = dot(jnp.concatenate(split(filt), axis=0), mirror, NN)
        filt = filt[:per] + filt[per:]
        turned = dot(mirror, mixed, NT).astype(BF16)
        lags = []
        for f in range(per):
            mine = slice(f * members, (f + 1) * members)
            wide = jnp.broadcast_to(filt[f : f + 1, :], (LANES, LANES))
            wide = pltpu.roll(wide, 1, 1, stride=1, stride_axis=0)
            hi, lo = split(jnp.where(causal, wide, 0.0))
            twice = jnp.concatenate([gate[mine], gate[mine]], axis=1)
            conv_ref[pl.ds(to + f * members, members), :] = dot(
                twice, jnp.concatenate([hi, lo], axis=0), NN
            )
            corr = jnp.where(mirrored_causal, dot(turned[:, mine], gate[mine], NN), 0.0)
            corr = pltpu.roll(corr, 1, 1, stride=1, stride_axis=0)
            lags.append(jnp.sum(corr, axis=0, keepdims=True))
        lag_hi, lag_lo = split(jnp.concatenate(lags, axis=0))
        lags = jnp.concatenate(
            [
                jnp.concatenate([lag_hi, lag_hi], axis=1),
                jnp.concatenate([lag_lo, jnp.zeros_like(lag_lo)], axis=1),
            ],
            axis=0,
        )
        for which, table in enumerate((head, der)):
            out = dot(lags, table, NN)
            out = jnp.where(own, out[:per] + out[per:], 0.0)
            out = jnp.sum(out, axis=0, keepdims=True)
            sums_ref[i, 2 * which : 2 * which + 1, :] = out[:, :LANES]
            sums_ref[i, 2 * which + 1 : 2 * which + 2, :] = out[:, LANES:]


def cross_kernel(
    members, modes, calls, mine_ref, other_ref, near_ref, more_ref, factor_ref, re_ref, im_ref,
    *refs,
):
    convs, out_ref = refs[:calls], refs[calls]
    per = LANES // modes
    size = per * members
    half = mine_ref.shape[0]
    is_up = lax.axis_index("seq") % 2 == 1
    lane = (lax.broadcasted_iota(jnp.int32, (members, 2 * LANES), 1) % LANES) // modes
    first = 0
    for conv_ref in convs:
        for i in range(conv_ref.shape[0] // size):
            g = first + i
            back_re, back_im = powers(re_ref, im_ref, g, True)
            rr, ri = re_ref[g, 32:33, :], im_ref[g, 32:33, :]
            coef_re, coef_im = complex_product(rr, ri, back_re, back_im)
            coef_hi, coef_lo = split(jnp.concatenate([coef_re, -coef_im], axis=1))
            k = g % half
            mine, other = pair(mine_ref, k), pair(other_ref, k)
            into = pick(is_up, other, mine) if g < half else pick(is_up, mine, other)
            own = pair(near_ref, k) if g < half else pair(more_ref, 2 * half + k)
            p = (factor_ref[0, 0, g : g + 1, :], factor_ref[0, 1, g : g + 1, :])
            yin = pick(is_up, into, plus(own, complex_product(*p, *into)))
            yin = jnp.concatenate(yin, axis=1)
            wide = jnp.concatenate([jnp.where(lane == f, yin, 0.0) for f in range(per)], axis=0)
            both = dot(
                jnp.concatenate(split(wide), axis=0),
                jnp.concatenate([coef_hi, coef_lo], axis=0),
                NT,
            )
            total = both[:size, :LANES] + both[size:, :LANES] + both[:size, LANES:]
            out_ref[g * size : (g + 1) * size, :] = conv_ref[i * size : (i + 1) * size, :] + total
        first += conv_ref.shape[0] // size


def finish_kernel(pos_ref, grouped, k_ref, v_ref, gk_hbm, gv_hbm, natural, gk_ref, gv_ref, sems):
    channels = k_ref.shape[0]
    tile = 256

    @pl.loop(0, channels // tile)
    def _(i):
        for part in range(tile // LANES):
            block = i * (tile // LANES) + part
            base = pl.multiple_of(block * LANES, LANES)
            for u in range(LANES):
                natural[pl.ds(base + u, 1), :] = grouped[pl.ds(pos_ref[block, u], 1), :]
        at = pl.ds(pl.multiple_of(i * tile, tile), tile)
        conv = natural[at, :]
        gk_ref[at, :] = (conv * v_ref[at, :].astype(F32)).astype(BF16)
        gv_ref[at, :] = (conv * k_ref[at, :].astype(F32)).astype(BF16)
        pltpu.make_async_copy(gk_ref.at[at, :], gk_hbm.at[at, :], sems.at[0]).start()
        pltpu.make_async_copy(gv_ref.at[at, :], gv_hbm.at[at, :], sems.at[1]).start()

    pltpu.make_async_copy(gk_ref, gk_hbm, sems.at[0]).wait()
    pltpu.make_async_copy(gv_ref, gv_hbm, sems.at[1]).wait()


def product_kernel(a_ref, b_hbm, out_hbm, b_ref, out_ref, sems):
    rows = a_ref.shape[0] // 4
    parts = [pl.ds(i * rows, rows) for i in range(4)]
    loads = [
        pltpu.make_async_copy(b_hbm.at[at, :], b_ref.at[at, :], sems.at[i])
        for i, at in enumerate(parts)
    ]
    for load in loads:
        load.start()
    stores = []
    for i, at in enumerate(parts):
        loads[i].wait()
        out_ref[at, :] = (a_ref[at, :].astype(F32) * b_ref[at, :].astype(F32)).astype(BF16)
        stores.append(
            pltpu.make_async_copy(out_ref.at[at, :], out_hbm.at[at, :], sems.at[4 + i])
        )
        stores[-1].start()
    for store in stores:
        store.wait()


def params_kernel(
    per, length, total_ref, last_ref, rate_ref, twist_ref, res_ref, log_rate_ref, grad_twist_ref, grad_res_ref
):
    modes, filters = rate_ref.shape
    picks = block_picks(filters // per, per, modes)
    rate, twist = rate_ref[...], twist_ref[...]
    rho, angle, scale = mode_rates(rate, twist, length)
    a_re, a_im, w_re, w_im = from_groups(
        [total_ref[i] + last_ref[i] for i in range(4)], picks, per
    )
    r0, r1 = res_ref[0], res_ref[1]
    b_re, b_im = complex_product(r0 * scale, r1 * scale, w_re, w_im)
    slope = rho * jnp.exp(-2.0 * rho) / scale
    log_rate_ref[...] = (r0 * a_re - r1 * a_im) * slope - b_re * rho - b_im * angle
    grad_twist_ref[...] = -b_im * rho
    grad_res_ref[0] = scale * a_re
    grad_res_ref[1] = -scale * a_im


def vmem(n):
    return [pl.BlockSpec(memory_space=pltpu.VMEM)] * n


SMEM = pl.BlockSpec(memory_space=pltpu.SMEM)


def params(mebibytes):
    return pltpu.CompilerParams(vmem_limit_bytes=mebibytes << 20)


def pinned(value):
    return pltpu.with_memory_space_constraint(value, pltpu.HBM)


def swap(value, bit):
    count = lax.axis_size("seq")
    return lax.ppermute(value, "seq", [(i, i ^ bit) for i in range(count)])


def together(*values):
    return lax.optimization_barrier(values)


def body(grad_out, query, key, value, conv_out, channel_filter, decay_rate, twist, residues):
    channels, positions = grad_out.shape
    filters, modes = decay_rate.shape
    members = channels // filters
    per = LANES // modes
    groups = filters // per
    count = lax.axis_size("seq")
    me = lax.axis_index("seq")
    length = positions * count
    shape = jax.ShapeDtypeStruct
    half, quarter = groups // 2, groups // 4

    def state(*lead):
        return shape((*lead, 2, members, LANES), F32)

    rates, twists = decay_rate.T, twist.T
    poles = jnp.swapaxes(residues, 1, 2)
    number = len(factor_blocks(0, count))
    hbm = pl.BlockSpec(memory_space=pltpu.HBM)
    wide = (channels, positions)
    blocks = (channels // LANES, LANES)
    table_shape = (groups, 40, LANES)
    (
        gate, mixed, y_lo, y_hi, x_lo, x_hi, ahead, pos, tab_re, tab_im, factors,
        own_out, own_key, own_value,
    ) = pl.pallas_call(
        functools.partial(states_kernel, members, modes, count),
        out_shape=(
            shape(wide, BF16), shape(wide, BF16), *[state(half)] * 4, state(groups),
            shape(blocks, jnp.int32), shape(table_shape, F32), shape(table_shape, F32),
            shape((number, 2, groups, LANES), F32), *[shape(wide, BF16)] * 3,
        ),
        in_specs=[hbm] * 8,
        out_specs=tuple(vmem(8) + [hbm] * 2 + vmem(4)),
        scratch_shapes=[
            pltpu.VMEM(blocks, jnp.int32), pltpu.VMEM((modes, filters), F32),
            pltpu.VMEM((modes, filters), F32), pltpu.VMEM((2, modes, filters), F32),
            pltpu.VMEM(wide, BF16), *[pltpu.VMEM(wide, F32)] * 2,
            *[pltpu.VMEM(table_shape, F32)] * 2, pltpu.SMEM(blocks, jnp.int32),
            pltpu.SemaphoreType.DMA((3,)), pltpu.SemaphoreType.DMA((4, 1 + CHUNKS)),
        ],
        compiler_params=params(20),
    )(
        *(
            pinned(part)
            for part in (
                channel_filter.reshape(blocks), rates, twists, poles,
                grad_out, query, key, value,
            )
        )
    )

    size = per * members

    def conv_call(first, number):
        return pl.pallas_call(
            functools.partial(conv_kernel, members, modes, first, UNROLL.get(number, 1)),
            out_shape=(shape((number * size, positions), F32), shape((number, 4, LANES), F32)),
            in_specs=vmem(4),
            out_specs=tuple(vmem(2)),
            compiler_params=params(8),
            cost_estimate=pl.CostEstimate(
                flops=number * COST, bytes_accessed=number << 10, transcendentals=0
            ),
        )(gate, mixed, tab_re, tab_im)

    def merge(level, *args):
        n = half >> level
        if level == 0:
            outs = (*[state(n // 2)] * 4, state(n))
        else:
            outs = (state(2, n),)
        return pl.pallas_call(
            functools.partial(merge_kernel, level),
            out_shape=outs,
            in_specs=vmem(6),
            out_specs=tuple(vmem(len(outs))),
            compiler_params=params(8),
        )(*args, factors)

    def rate_merge(level, *args):
        n = half >> level
        sums = shape((4, n, LANES), F32)
        if level == 0:
            outs = (*[state(n // 2)] * 4, state(n + n // 2), sums)
        else:
            outs = (state(2, n), sums)
        return pl.pallas_call(
            functools.partial(rate_merge_kernel, level),
            out_shape=outs,
            in_specs=vmem(len(args)),
            out_specs=tuple(vmem(len(outs))),
            compiler_params=params(8),
        )(*args)

    got0 = swap(ahead, 1)
    ty_lo, ty_hi, tx_lo, tx_hi, ahead1 = merge(0, y_lo, y_hi, x_lo, x_hi, got0)
    ahead1, gate, mixed = together(ahead1, gate, mixed)
    got1 = swap(ahead1, 2)
    vw = pl.pallas_call(
        functools.partial(rates_kernel, members, modes),
        out_shape=(*[state(half)] * 4, state(groups + half)),
        in_specs=vmem(5),
        out_specs=tuple(vmem(5)),
        compiler_params=params(8),
        cost_estimate=pl.CostEstimate(flops=2 * COST, bytes_accessed=1 << 10, transcendentals=0),
    )(gate, mixed, tab_re, tab_im, y_hi)
    parts = [5, 5, groups - 10]
    made = [conv_call(0, parts[0])]
    got1, vw, made[0] = together(got1, vw, made[0])
    more0 = swap(vw[4], 1)
    (yx,) = merge(1, ty_lo, ty_hi, tx_lo, tx_hi, got1)

    base = 4
    bit, at = base, 2
    tot, sent, into = yx, yx, ()
    while bit < count:
        last, next_last = bit * 2 >= count, bit * 4 >= count
        sent, gate, mixed = together(sent, gate, mixed)
        got = swap(sent, bit)
        if bit == base:
            rate0 = rate_merge(
                0, y_lo, y_hi, x_lo, x_hi, got0, *vw[:4], more0, factors, ty_hi
            )
            more1, gate, mixed = together(rate0[4], gate, mixed)
            more1 = swap(more1, 2)
        if bit == base or last:
            first = sum(parts[: len(made)])
            conv = conv_call(first, groups - first if last else parts[len(made)])
            if last:
                rate1 = rate_merge(
                    1, ty_lo, ty_hi, tx_lo, tx_hi, got1, *rate0[:4], more1, factors
                )
                got, rate1 = together(got, rate1)
            got, conv = together(got, conv)
            made.append(conv)
        outs = [state(quarter)] * 2
        if not last:
            outs.append(state(2, quarter))
            if next_last:
                outs.append(state(1, quarter))
        outs = pl.pallas_call(
            functools.partial(scan_kernel, bit == base, last, next_last, bit, at),
            out_shape=tuple(outs),
            in_specs=vmem(3 + len(into)),
            out_specs=tuple(vmem(len(outs))),
            compiler_params=params(4),
        )(tot, got, factors, *into)
        into = outs[:2]
        if not last:
            tot, sent = outs[2], outs[-1]
        bit *= 2
        at += 2
    into_y, into_x = into
    convs, lags = zip(*made)
    calls = len(convs)
    total = pl.pallas_call(
        functools.partial(total_kernel, calls),
        out_shape=shape((4, groups, LANES), F32),
        in_specs=vmem(7 + calls),
        out_specs=vmem(1)[0],
        compiler_params=params(8),
    )(yx, rate1[0], into_y, into_x, factors, rate0[5], rate1[1], *lags)

    def add(a, b):
        return pl.pallas_call(
            add_kernel,
            out_shape=shape((4, groups, LANES), F32),
            in_specs=vmem(2),
            out_specs=vmem(1)[0],
            compiler_params=params(2),
        )(a, b)

    into_y, total = together(into_y, total)
    other = swap(into_y, 2)
    total = add(total, swap(total, 1))
    total, own_out = together(total, own_out)
    got = swap(total, 2)
    grad_query = pl.pallas_call(
        product_kernel,
        out_shape=shape(wide, BF16),
        in_specs=vmem(1) + [hbm],
        out_specs=hbm,
        scratch_shapes=[pltpu.VMEM(wide, BF16)] * 2 + [pltpu.SemaphoreType.DMA((8,))],
        compiler_params=params(8),
        cost_estimate=pl.CostEstimate(flops=COST, bytes_accessed=1 << 10, transcendentals=0),
    )(own_out, pinned(conv_out))
    other, grad_query = together(other, grad_query)
    chip = pl.pallas_call(
        down_kernel,
        out_shape=state(half),
        in_specs=vmem(5),
        out_specs=vmem(1)[0],
        compiler_params=params(4),
    )(into_y, other, got1, more1, factors)
    total = add(total, got)
    total, chip = together(total, chip)
    got = swap(total, 4)
    chip_other = swap(chip, 1)
    cost = pl.CostEstimate(flops=COST, bytes_accessed=1 << 10, transcendentals=0)
    grouped = pl.pallas_call(
        functools.partial(cross_kernel, members, modes, calls),
        out_shape=shape(wide, F32),
        in_specs=vmem(7 + calls),
        out_specs=vmem(1)[0],
        compiler_params=params(12),
        cost_estimate=cost,
    )(chip, chip_other, got0, more0, factors, tab_re, tab_im, *convs)
    got, grouped = together(got, grouped)
    total = add(total, got)
    bit = 8
    while bit * 2 < count:
        total = add(total, swap(total, bit))
        bit *= 2
    total, grouped = together(total, grouped)
    got = swap(total, bit)
    grad_key, grad_value = pl.pallas_call(
        finish_kernel,
        out_shape=(shape(wide, BF16), shape(wide, BF16)),
        in_specs=[SMEM] + vmem(3),
        out_specs=(hbm, hbm),
        scratch_shapes=[pltpu.VMEM(wide, F32)] + [pltpu.VMEM(wide, BF16)] * 2
        + [pltpu.SemaphoreType.DMA((2,))],
        compiler_params=params(12),
        cost_estimate=cost,
    )(pos, grouped, own_key, own_value)
    got, grad_key, grad_value = together(got, grad_key, grad_value)
    one = shape((modes, filters), F32)
    log_rate, grad_twist, grad_res = pl.pallas_call(
        functools.partial(params_kernel, per, float(length)),
        out_shape=(one, one, shape((2, modes, filters), F32)),
        in_specs=vmem(5),
        out_specs=tuple(vmem(3)),
        compiler_params=params(4),
    )(total, got, rates, twists, poles)
    return (
        grad_query, grad_key, grad_value, log_rate.T, grad_twist.T, jnp.swapaxes(grad_res, 1, 2)
    )


def solution(mesh):
    wide = P(None, ("groups", "seq"))
    return jax.shard_map(
        body,
        mesh=mesh,
        in_specs=(wide,) * 5 + (P(),) * 4,
        out_specs=(wide, wide, wide, P("groups", None), P("groups", None), P("groups", None, None)),
        check_vma=False,
    )
```
